256 devices in a mesh: pair: 128 (over x, y, z_lo, core), aux: 2 (over z_hi).
Axes of the slice: x: 4, y: 4, z: 8 (z_hi: 2, z_lo: 4; z = z_hi * 4 + z_lo), core: 2. Of those that a mesh axis runs over, the one named last changes fastest.
Arguments:
- amplitudes: bfloat16 [256, 512, 512], P(None, 'pair'), may hold values from -6 to 6
- ladder: bfloat16 [256, 256], replicated, may hold values from -0.375 to 0.375
- cholesky: bfloat16 [16, 512, 512], P('aux'), may hold values from -0.25 to 0.25
- pair_ids: int32 [256], P('pair'), may hold values from 0 to 255, each once
- occ_energy: float32 [16], replicated, may hold values from -2 to -0.5
- vir_energy: float32 [512], replicated, may hold values from 0.5 to 3
Outputs:
- update: float32 [256, 512, 512], P('pair', None, 'aux')
The draws below stay inside these ranges and needn't reach their ends.
Inputs may be any that keep to these rules, and one draw needn't show every extreme that they name: `pair_ids`: every value 0 to 255 appears once.
All inputs are finite; a program needn't handle non-finite values.
Results may differ from the reference program's by a relative error of at most 0.0029.
Values may be sent and summed in bfloat16 or wider, within the bound.
No kernel may reach another device: no remote copies, remote signals or barrier semaphores. Data moves between devices by JAX's collectives and lax.ppermute only.
A program may use at most 64 MiB of HBM per device.

```python
import jax
import jax.numpy as jnp
from jax import lax

NO = 16
NV = 512
OP = 256
NQ = 16


def block_scale(key, shape, pieces, low, top_value):
    def one(dim, shards_of):
        draws = jax.random.uniform(jax.random.fold_in(jax.random.fold_in(key, 6), dim), (shards_of,), jnp.float32, low / len(pieces), top_value / len(pieces))
        return jnp.repeat(jnp.exp(draws), shape[dim] // shards_of).reshape((-1,) + (1,) * (len(shape) - dim - 1))

    level = one(*pieces[0])
    for cut in pieces[1:]:
        level = level * one(*cut)
    return level


def centred(rng, extent, spread, most, split=(), dtype=jnp.bfloat16):
    entries = spread * jax.random.normal(rng, extent, jnp.float32)
    if split:
        entries = entries * block_scale(rng, extent, split, -0.22, 0.18)
    return jnp.clip(entries, -most, most).astype(dtype)


def setup_inputs(seed: int = 0) -> dict:
    seeds = jax.random.split(jax.random.key(seed), 7)
    return {
        "amplitudes": centred(seeds[0], (OP, NV, NV), 1.0, 6.0, ((1, 128),)),
        "ladder": centred(seeds[1], (OP, OP), OP ** -0.5, 0.375),
        "cholesky": centred(seeds[2], (NQ, NV, NV), NV ** -0.5, 0.25, ((0, 2),)),
        "pair_ids": jax.random.permutation(seeds[3], OP).astype(jnp.int32),
        "occ_energy": jnp.clip(jax.random.uniform(seeds[4], (NO,), jnp.float32, -2.0, -0.5), -2.0, -0.5),
        "vir_energy": jnp.clip(jax.random.uniform(seeds[5], (NV,), jnp.float32, 0.5, 3.0), 0.5, 3.0),
    }


def reference(amplitudes, ladder, cholesky, pair_ids, occ_energy, vir_energy):
    flat_amps = amplitudes.reshape(OP, NV * NV)
    hole_term = jnp.dot(ladder, flat_amps, preferred_element_type=jnp.float32).astype(jnp.bfloat16)
    hole_term = hole_term.reshape(OP, NV, NV)
    by_first = jnp.transpose(amplitudes, (1, 0, 2)).reshape(NV, OP * NV)

    def add_vector(running, vector):
        mixed_terms = jnp.dot(vector, by_first, preferred_element_type=jnp.float32).astype(jnp.bfloat16)
        mixed_terms = jnp.transpose(mixed_terms.reshape(NV, OP, NV), (1, 0, 2)).reshape(OP * NV, NV)
        product = jnp.dot(mixed_terms, vector.T, preferred_element_type=jnp.float32)
        return running + product.reshape(OP, NV, NV), None

    particle, _ = lax.scan(add_vector, jnp.zeros((OP, NV, NV), jnp.float32), cholesky)
    first_occ = (pair_ids // NO).astype(jnp.int32)
    second_occ = (pair_ids % NO).astype(jnp.int32)
    occ_sum = occ_energy[first_occ] + occ_energy[second_occ]
    denominator = vir_energy[None, :, None] + vir_energy[None, None, :] - occ_sum[:, None, None]
    return (hole_term.astype(jnp.float32) + particle) / denominator
```

```python
import jax
import jax.numpy as jnp
from jax import lax
from jax.sharding import PartitionSpec as P

NO = 16


def denominators(pair_ids, occ_energy, vir_rows, vir_cols):
    orbitals = jnp.arange(NO, dtype=jnp.int32)
    first_hot = (pair_ids[:, None] // NO == orbitals[None, :]).astype(jnp.float32)
    second_hot = (pair_ids[:, None] % NO == orbitals[None, :]).astype(jnp.float32)
    occ_sum = jnp.sum((first_hot + second_hot) * occ_energy[None, :], axis=1)
    return vir_rows[None, :, None] + vir_cols[None, None, :] - occ_sum[:, None, None]


def shards(amplitudes, ladder, cholesky, pair_ids, occ_energy, vir_energy):
    n_virt = amplitudes.shape[2]
    rows = amplitudes.shape[1]
    half_width = n_virt // lax.axis_size("aux")
    aux_index = lax.axis_index("aux")
    mine = aux_index * half_width
    amp_half = lax.dynamic_slice_in_dim(amplitudes, mine, half_width, 2)
    hole_half = jnp.dot(
        ladder, amp_half.reshape(amp_half.shape[0], -1), preferred_element_type=jnp.float32
    ).astype(jnp.bfloat16).reshape(-1, rows, half_width)
    pair_amps = lax.all_to_all(amplitudes, "pair", split_axis=0, concat_axis=1, tiled=True)
    pair_hole = lax.all_to_all(hole_half, "pair", split_axis=0, concat_axis=1, tiled=True)
    mixed = jnp.einsum(
        "qac,pcd->qpad", cholesky, pair_amps, preferred_element_type=jnp.float32
    ).astype(jnp.bfloat16)
    other_cols = lax.dynamic_slice_in_dim(cholesky, half_width - mine, half_width, 1)
    own_cols = lax.dynamic_slice_in_dim(cholesky, mine, half_width, 1)
    theirs = jnp.einsum("qpad,qbd->pab", mixed, other_cols, preferred_element_type=jnp.float32)
    received = lax.ppermute(theirs.astype(jnp.bfloat16), "aux", [(0, 1), (1, 0)])
    own = jnp.einsum("qpad,qbd->pab", mixed, own_cols, preferred_element_type=jnp.float32)
    vir_cols = lax.dynamic_slice_in_dim(vir_energy, mine, half_width, 0)
    denominator = denominators(pair_ids, occ_energy, vir_energy, vir_cols)
    total = pair_hole.astype(jnp.float32) + own + received.astype(jnp.float32)
    return total / denominator


def solution(mesh):
    in_specs = (P(None, "pair", None), P(), P("aux", None, None), P("pair"), P(), P())
    out_specs = P("pair", None, "aux")
    return jax.shard_map(shards, mesh=mesh, in_specs=in_specs, out_specs=out_specs, check_vma=False)
```

```python
import jax
import jax.numpy as jnp
from jax import lax
from jax.experimental import pallas as pl
from jax.experimental.pallas import tpu as pltpu
from jax.sharding import Mesh, PartitionSpec as P

NO = 16
AXES = ("x", "y", "z", "core", "aux")
PAIR = AXES[:4]
VMEM_LIMIT = 24 * 1024 * 1024
NT = (((1,), (1,)), ((), ()))


def add_vector(vector, cols, amps_ref, total_ref):
    turned = [
        lax.dot_general(amps_ref[p], cols, NT, preferred_element_type=jnp.float32).astype(jnp.bfloat16)
        for p in range(amps_ref.shape[0])
    ]
    total_ref[...] += jnp.dot(
        vector, jnp.concatenate(turned, axis=1), preferred_element_type=jnp.float32
    )


def own_kernel(place_ref, amps_ref, vec_ref, total_ref):
    half = total_ref.shape[1] // 2

    @pl.when(pl.program_id(0) == 0)
    def _():
        total_ref[...] = jnp.zeros_like(total_ref)

    start = pl.multiple_of(place_ref[0] * half, half)
    add_vector(vec_ref[0], vec_ref[0, pl.ds(start, half), :], amps_ref, total_ref)


def own_vectors(place, amps, cholesky):
    nq, nv, _ = cholesky.shape
    return pl.pallas_call(
        own_kernel,
        grid_spec=pltpu.PrefetchScalarGridSpec(
            num_scalar_prefetch=1,
            grid=(nq,),
            in_specs=[
                pl.BlockSpec(amps.shape, lambda q, _: (0, 0, 0)),
                pl.BlockSpec((1, nv, nv), lambda q, _: (q, 0, 0)),
            ],
            out_specs=pl.BlockSpec((nv, nv), lambda q, _: (0, 0)),
        ),
        out_shape=jax.ShapeDtypeStruct((nv, nv), jnp.float32),
        compiler_params=pltpu.CompilerParams(vmem_limit_bytes=VMEM_LIMIT),
        cost_estimate=pl.CostEstimate(
            flops=4 * nq * nv**3, bytes_accessed=2 * nq * nv * nv, transcendentals=0
        ),
        name="own_vectors",
    )(place, amps, cholesky)


def other_kernel(
    place_ref, occ_ref, amps_ref, near0, far0, near1, far1, base_ref, hole_ref, rows_ref, cols_ref, out_ref, vec, total, sems
):
    nq, slots, strip, nv = vec.shape
    half = nv // 2
    core, first = place_ref[1], (place_ref[2], place_ref[3])
    part = nq // 2

    for h, sources in enumerate(((near0, far0), (near1, far1))):
        for side, src in enumerate(sources):
            base = (core if side == 0 else 1 - core) * (slots // 2)
            for outer in range(4):
                for inner in range(4):
                    dx, dy = (inner, outer) if h == 0 else (outer, inner)
                    x = lax.rem(first[0] + 4 - dx, 4)
                    y = lax.rem(first[1] + 4 - dy, 4)
                    pltpu.make_async_copy(
                        src.at[outer, inner],
                        vec.at[pl.ds(h * part, part), base + x * 4 + y],
                        sems.at[h],
                    ).start()
    total[...] = base_ref[...]
    for q in range(nq):
        if q % part == 0:
            block = vec.at[pl.ds(q, part)]
            pltpu.make_async_copy(block, block, sems.at[q // part]).wait()
        cols = vec[q, pl.ds(place_ref[0] * (slots // 2), slots // 2)].reshape(half, nv)
        add_vector(vec[q].reshape(nv, nv), cols, amps_ref, total)
    level = rows_ref[...] + cols_ref[...]
    for p in range(out_ref.shape[0]):
        value = hole_ref[p].astype(jnp.float32) + total[:, p * half : (p + 1) * half]
        out_ref[p] = value / (level - occ_ref[p])


def other_vectors(place, occ_sum, amps, gathered, base, hole, rows, cols):
    part, strip, nv = gathered[0].shape[2:]
    nq = 2 * part
    vmem = pl.BlockSpec(memory_space=pltpu.VMEM)
    smem = pl.BlockSpec(memory_space=pltpu.SMEM)
    anywhere = pl.BlockSpec(memory_space=pl.ANY)
    return pl.pallas_call(
        other_kernel,
        in_specs=[smem, smem, vmem, *[anywhere] * 4, vmem, vmem, vmem, vmem],
        out_specs=vmem,
        out_shape=jax.ShapeDtypeStruct(hole.shape, jnp.float32),
        scratch_shapes=[
            pltpu.VMEM((nq, nv // strip, strip, nv), jnp.bfloat16),
            pltpu.VMEM((nv, nv), jnp.float32),
            pltpu.SemaphoreType.DMA((2,)),
        ],
        compiler_params=pltpu.CompilerParams(vmem_limit_bytes=VMEM_LIMIT),
        cost_estimate=pl.CostEstimate(
            flops=4 * nq * nv**3, bytes_accessed=2 * nq * nv * nv, transcendentals=0
        ),
        name="other_vectors",
    )(place, occ_sum, amps, *gathered, base, hole, rows, cols)


def gather_axis(block, axis):
    return jnp.stack(
        [block] + [lax.ppermute(block, axis, [(i, (i + d) % 4) for i in range(4)]) for d in (1, 2, 3)]
    )


def shards(amplitudes, ladder, cholesky, pair_ids, occ_energy, vir_energy):
    rows, n_virt = amplitudes.shape[1:]
    half_width = n_virt // lax.axis_size("aux")
    aux_index, core = lax.axis_index("aux"), lax.axis_index("core")
    planes = lax.axis_size("x") * lax.axis_size("y")
    strip = half_width // planes
    mine = aux_index * half_width

    slot = core * planes + lax.axis_index("x") * lax.axis_size("y") + lax.axis_index("y")
    piece = lax.dynamic_slice_in_dim(cholesky, slot * strip, strip, 1)
    piece = lax.ppermute(piece, "aux", [(0, 1), (1, 0)])
    gathered = []
    part = piece.shape[0] // 2
    for h, order in enumerate((("x", "y"), ("y", "x"))):
        near = piece[h * part : (h + 1) * part]
        for axis in order:
            near = gather_axis(near, axis)
        gathered += [near, lax.ppermute(near, "core", [(0, 1), (1, 0)])]

    amp_half = lax.dynamic_slice_in_dim(amplitudes, mine, half_width, 2)
    hole_half = jnp.dot(
        ladder, amp_half.reshape(amp_half.shape[0], -1), preferred_element_type=jnp.float32
    ).astype(jnp.bfloat16).reshape(-1, rows, half_width)
    both = jnp.concatenate([amplitudes, hole_half], axis=2)
    both = lax.all_to_all(both, PAIR, split_axis=0, concat_axis=1, tiled=True)
    pair_amps, pair_hole = both[:, :, :n_virt], both[:, :, n_virt:]

    orbitals = jnp.arange(NO, dtype=jnp.int32)
    first_hot = (pair_ids[:, None] // NO == orbitals[None, :]).astype(jnp.float32)
    second_hot = (pair_ids[:, None] % NO == orbitals[None, :]).astype(jnp.float32)
    occ_sum = jnp.sum((first_hot + second_hot) * occ_energy[None, :], axis=1)
    vir_cols = lax.dynamic_slice_in_dim(vir_energy, mine, half_width, 0)
    place = jnp.stack([aux_index, core, lax.axis_index("x"), lax.axis_index("y")]).astype(jnp.int32)

    base = own_vectors(place, pair_amps, cholesky)
    return other_vectors(
        place, occ_sum, pair_amps, gathered, base, pair_hole, vir_energy[:, None], vir_cols[None, :]
    )


def solution(mesh):
    fine = Mesh(mesh.devices.reshape(4, 4, 4, 2, 2), AXES)
    in_specs = (P(None, PAIR, None), P(), P("aux", None, None), P(PAIR), P(), P())
    out_specs = P(PAIR, None, "aux")
    return jax.shard_map(shards, mesh=fine, in_specs=in_specs, out_specs=out_specs, check_vma=False)
```

```python
import jax
import jax.numpy as jnp
from jax import lax
from jax.experimental import pallas as pl
from jax.experimental.pallas import tpu as pltpu
from jax.sharding import Mesh, PartitionSpec as P

NO = 16
AXES = ("x", "y", "z", "core", "aux")
PAIR = AXES[:4]
VMEM_LIMIT = 24 * 1024 * 1024
NT = (((1,), (1,)), ((), ()))


def add_vector(vector, cols, amps_ref, total_ref):
    turned = [
        lax.dot_general(amps_ref[p], cols, NT, preferred_element_type=jnp.float32).astype(jnp.bfloat16)
        for p in range(amps_ref.shape[0])
    ]
    total_ref[...] += jnp.dot(
        vector, jnp.concatenate(turned, axis=1), preferred_element_type=jnp.float32
    )


def own_kernel(place_ref, amps_ref, vec_ref, total_ref, vec, sems):
    nq, nv, _ = vec.shape
    half = nv // 2
    copies = [pltpu.make_async_copy(vec_ref.at[q], vec.at[q], sems.at[q]) for q in range(nq)]
    for copy in copies:
        copy.start()
    total_ref[...] = jnp.zeros_like(total_ref)
    start = pl.multiple_of(place_ref[0] * half, half)
    for q in range(nq):
        copies[q].wait()
        add_vector(vec[q], vec[q, pl.ds(start, half), :], amps_ref, total_ref)


def own_vectors(place, amps, cholesky):
    nq, nv, _ = cholesky.shape
    return pl.pallas_call(
        own_kernel,
        in_specs=[
            pl.BlockSpec(memory_space=pltpu.SMEM),
            pl.BlockSpec(memory_space=pltpu.VMEM),
            pl.BlockSpec(memory_space=pltpu.HBM),
        ],
        out_specs=pl.BlockSpec(memory_space=pltpu.VMEM),
        out_shape=jax.ShapeDtypeStruct((nv, nv), jnp.float32),
        scratch_shapes=[pltpu.VMEM((nq, nv, nv), jnp.bfloat16), pltpu.SemaphoreType.DMA((nq,))],
        compiler_params=pltpu.CompilerParams(vmem_limit_bytes=VMEM_LIMIT),
        cost_estimate=pl.CostEstimate(
            flops=4 * nq * nv**3, bytes_accessed=2 * nq * nv * nv, transcendentals=0
        ),
        name="own_vectors",
    )(place, amps, cholesky)


def other_kernel(
    place_ref, occ_ref, amps_ref, near0, far0, near1, far1, base_ref, hole_ref, rows_ref, cols_ref, out_ref, vec, total, sems
):
    nq, slots, strip, nv = vec.shape
    half = nv // 2
    core, first = place_ref[1], (place_ref[2], place_ref[3])
    part = nq // 2

    for h, sources in enumerate(((near0, far0), (near1, far1))):
        for side, src in enumerate(sources):
            base = (core if side == 0 else 1 - core) * (slots // 2)
            for outer in range(4):
                for inner in range(4):
                    dx, dy = (inner, outer) if h == 0 else (outer, inner)
                    x = lax.rem(first[0] + 4 - dx, 4)
                    y = lax.rem(first[1] + 4 - dy, 4)
                    pltpu.make_async_copy(
                        src.at[outer, inner],
                        vec.at[pl.ds(h * part, part), base + x * 4 + y],
                        sems.at[h],
                    ).start()
    total[...] = base_ref[...]
    for q in range(nq):
        if q % part == 0:
            block = vec.at[pl.ds(q, part)]
            pltpu.make_async_copy(block, block, sems.at[q // part]).wait()
        cols = vec[q, pl.ds(place_ref[0] * (slots // 2), slots // 2)].reshape(half, nv)
        add_vector(vec[q].reshape(nv, nv), cols, amps_ref, total)
    level = rows_ref[...] + cols_ref[...]
    for p in range(out_ref.shape[0]):
        side = slice(p * half, (p + 1) * half)
        out_ref[p] = (hole_ref[:, side].astype(jnp.float32) + total[:, side]) / (level - occ_ref[p])


def other_vectors(place, occ_sum, amps, gathered, base, hole, rows, cols):
    part, strip, nv = gathered[0].shape[2:]
    nq = 2 * part
    vmem = pl.BlockSpec(memory_space=pltpu.VMEM)
    smem = pl.BlockSpec(memory_space=pltpu.SMEM)
    anywhere = pl.BlockSpec(memory_space=pl.ANY)
    return pl.pallas_call(
        other_kernel,
        in_specs=[smem, smem, vmem, *[anywhere] * 4, vmem, vmem, vmem, vmem],
        out_specs=vmem,
        out_shape=jax.ShapeDtypeStruct((amps.shape[0], nv, nv // 2), jnp.float32),
        scratch_shapes=[
            pltpu.VMEM((nq, nv // strip, strip, nv), jnp.bfloat16),
            pltpu.VMEM((nv, nv), jnp.float32),
            pltpu.SemaphoreType.DMA((2,)),
        ],
        compiler_params=pltpu.CompilerParams(vmem_limit_bytes=VMEM_LIMIT),
        cost_estimate=pl.CostEstimate(
            flops=4 * nq * nv**3, bytes_accessed=2 * nq * nv * nv, transcendentals=0
        ),
        name="other_vectors",
    )(place, occ_sum, amps, *gathered, base, hole, rows, cols)


def gather_axis(block, axis):
    return jnp.stack(
        [block] + [lax.ppermute(block, axis, [(i, (i + d) % 4) for i in range(4)]) for d in (1, 2, 3)]
    )


def shards(amplitudes, ladder, cholesky, pair_ids, occ_energy, vir_energy):
    n_pair, rows, n_virt = amplitudes.shape
    half_width = n_virt // lax.axis_size("aux")
    aux_index, core = lax.axis_index("aux"), lax.axis_index("core")
    planes = lax.axis_size("x") * lax.axis_size("y")
    strip = half_width // planes
    mine = aux_index * half_width
    each = pair_ids.shape[0]
    peers = n_pair // each

    slot = core * planes + lax.axis_index("x") * lax.axis_size("y") + lax.axis_index("y")
    piece = lax.dynamic_slice_in_dim(cholesky, slot * strip, strip, 1)
    piece = lax.ppermute(piece, "aux", [(0, 1), (1, 0)])

    amp_half = lax.dynamic_slice_in_dim(amplitudes, mine, half_width, 2)
    hole_half = jnp.dot(
        ladder, amp_half.reshape(n_pair, -1), preferred_element_type=jnp.float32
    ).astype(jnp.bfloat16)
    hole_half = hole_half.reshape(peers, each, rows, half_width).transpose(0, 2, 1, 3)
    both = jnp.concatenate(
        [amplitudes.reshape(peers, each, rows, n_virt), hole_half.reshape(peers, 1, rows, n_virt)], axis=1
    )
    both, piece = lax.optimization_barrier((both, piece))
    both = lax.all_to_all(both, PAIR, split_axis=0, concat_axis=0, tiled=True)

    gathered = []
    part = piece.shape[0] // 2
    for h, order in enumerate((("x", "y"), ("y", "x"))):
        near = piece[h * part : (h + 1) * part]
        for axis in order:
            near = gather_axis(near, axis)
        gathered += [near, lax.ppermute(near, "core", [(0, 1), (1, 0)])]

    both = both.transpose(1, 0, 2, 3).reshape(each + 1, n_virt, n_virt)
    pair_amps, pair_hole = both[:each], both[each]

    orbitals = jnp.arange(NO, dtype=jnp.int32)
    first_hot = (pair_ids[:, None] // NO == orbitals[None, :]).astype(jnp.float32)
    second_hot = (pair_ids[:, None] % NO == orbitals[None, :]).astype(jnp.float32)
    occ_sum = jnp.sum((first_hot + second_hot) * occ_energy[None, :], axis=1)
    vir_cols = lax.dynamic_slice_in_dim(vir_energy, mine, half_width, 0)
    place = jnp.stack([aux_index, core, lax.axis_index("x"), lax.axis_index("y")]).astype(jnp.int32)

    base = own_vectors(place, pair_amps, cholesky)
    return other_vectors(
        place, occ_sum, pair_amps, gathered, base, pair_hole, vir_energy[:, None], vir_cols[None, :]
    )


def solution(mesh):
    fine = Mesh(mesh.devices.reshape(4, 4, 4, 2, 2), AXES)
    in_specs = (P(None, PAIR, None), P(), P("aux", None, None), P(PAIR), P(), P())
    out_specs = P(PAIR, None, "aux")
    return jax.shard_map(shards, mesh=fine, in_specs=in_specs, out_specs=out_specs, check_vma=False)
```

```python
import jax
import jax.numpy as jnp
from jax import lax
from jax.experimental import pallas as pl
from jax.experimental.pallas import tpu as pltpu
from jax.sharding import Mesh, PartitionSpec as P

NO = 16
AXES = ("x", "y", "z", "core", "aux")
PAIR = AXES[:4]
SIDE = 4
VMEM_LIMIT = 24 * 1024 * 1024
NT = (((1,), (1,)), ((), ()))


def add_vector(vector, cols, amps_ref, total_ref):
    nv = vector.shape[0]
    turned = lax.dot_general(amps_ref[...], cols, NT, preferred_element_type=jnp.float32).astype(jnp.bfloat16)
    total_ref[...] += jnp.dot(
        vector, jnp.concatenate([turned[:nv], turned[nv:]], axis=1), preferred_element_type=jnp.float32
    )


def own_kernel(place_ref, amps_ref, vec_ref, total_ref, vec, sems):
    nq, nv, _ = vec.shape
    half = nv // 2
    copies = [pltpu.make_async_copy(vec_ref.at[q], vec.at[q], sems.at[q]) for q in range(nq)]
    for copy in copies:
        copy.start()
    total_ref[...] = jnp.zeros_like(total_ref)
    start = pl.multiple_of(place_ref[0] * half, half)
    for q in range(nq):
        copies[q].wait()
        add_vector(vec[q], vec[q, pl.ds(start, half), :], amps_ref, total_ref)


def estimate(nq, nv):
    return pl.CostEstimate(flops=4 * nq * nv**3, bytes_accessed=2 * nq * nv * nv, transcendentals=0)


def own_vectors(place, amps, cholesky):
    nq, nv, _ = cholesky.shape
    return pl.pallas_call(
        own_kernel,
        in_specs=[
            pl.BlockSpec(memory_space=pltpu.SMEM),
            pl.BlockSpec(memory_space=pltpu.VMEM),
            pl.BlockSpec(memory_space=pltpu.HBM),
        ],
        out_specs=pl.BlockSpec(memory_space=pltpu.VMEM),
        out_shape=jax.ShapeDtypeStruct((nv, nv), jnp.float32),
        scratch_shapes=[pltpu.VMEM((nq, nv, nv), jnp.bfloat16), pltpu.SemaphoreType.DMA((nq,))],
        compiler_params=pltpu.CompilerParams(vmem_limit_bytes=VMEM_LIMIT),
        cost_estimate=estimate(16 * nq, nv),
        name="own_vectors",
    )(place, amps, cholesky)


def other_kernel(
    place_ref, occ_ref, amps_ref, near_ref, far_ref, base_ref, hole_ref, rows_ref, cols_ref, out_ref, vec, total, sems
):
    nq, slots, strip, nv = vec.shape
    half, part = nv // 2, nq // 2
    core, x0, y0 = place_ref[1], place_ref[2], place_ref[3]

    for h in range(2):
        for owner, src in ((core, near_ref), (1 - core, far_ref)):
            for outer in range(SIDE):
                for inner in range(SIDE):
                    dx = inner + owner * (outer - inner)
                    dy = outer + owner * (inner - outer)
                    x, y = lax.rem(x0 + SIDE - dx, SIDE), lax.rem(y0 + SIDE - dy, SIDE)
                    pltpu.make_async_copy(
                        src.at[outer, inner, pl.ds(h * part, part)],
                        vec.at[pl.ds(h * part, part), (owner * SIDE + x) * SIDE + y],
                        sems.at[h],
                    ).start()
    total[...] = base_ref[...]
    for q in range(nq):
        if q % part == 0:
            block = vec.at[pl.ds(q, part)]
            pltpu.make_async_copy(block, block, sems.at[q // part]).wait()
        cols = vec[q, pl.ds(place_ref[0] * (slots // 2), slots // 2)].reshape(half, nv)
        add_vector(vec[q].reshape(nv, nv), cols, amps_ref, total)
    level = rows_ref[...] + cols_ref[...]
    for p in range(out_ref.shape[0]):
        value = hole_ref[p].astype(jnp.float32) + total[:, p * half : (p + 1) * half]
        out_ref[p] = value / (level - occ_ref[p])


def other_vectors(place, occ_sum, amps, near, far, base, hole, rows, cols):
    nq, strip, nv = near.shape[2:]
    vmem = pl.BlockSpec(memory_space=pltpu.VMEM)
    smem = pl.BlockSpec(memory_space=pltpu.SMEM)
    anywhere = pl.BlockSpec(memory_space=pl.ANY)
    return pl.pallas_call(
        other_kernel,
        in_specs=[smem, smem, vmem, anywhere, anywhere, vmem, vmem, vmem, vmem],
        out_specs=vmem,
        out_shape=jax.ShapeDtypeStruct(hole.shape, jnp.float32),
        scratch_shapes=[
            pltpu.VMEM((nq, nv // strip, strip, nv), jnp.bfloat16),
            pltpu.VMEM((nv, nv), jnp.float32),
            pltpu.SemaphoreType.DMA((2,)),
        ],
        compiler_params=pltpu.CompilerParams(vmem_limit_bytes=VMEM_LIMIT),
        cost_estimate=estimate(nq, nv),
        name="other_vectors",
    )(place, occ_sum, amps, near, far, base, hole, rows, cols)


def plane_shift(block, shift, first_core_axis):
    pairs = []
    for x in range(SIDE):
        for y in range(SIDE):
            for core in range(2):
                if core == first_core_axis:
                    to = x * SIDE + (y + shift) % SIDE
                else:
                    to = (x + shift) % SIDE * SIDE + y
                pairs.append(((x * SIDE + y) * 2 + core, to * 2 + core))
    return lax.ppermute(block, ("x", "y", "core"), pairs)


def gather_plane(block):
    for stage in range(2):
        block = jnp.stack([block] + [plane_shift(block, d, 1 - stage) for d in (1, 2, 3)])
    return block


def ring_pairs(step):
    steps = {1: (1, 1), 3: (-1, -1), 2: (2, -2)}[step]
    pairs = []
    for z8 in range(2 * SIDE):
        for core in range(2):
            to = (z8 + steps[core]) % (2 * SIDE)
            pairs.append(((z8 % SIDE * 2 + core) * 2 + z8 // SIDE, (to % SIDE * 2 + core) * 2 + to // SIDE))
    return pairs


def ring_target(z8, core, step):
    move = {0: 0, 1: 1, 3: -1}.get(step)
    move = 2 - 4 * core if move is None else move
    return lax.rem(z8 + move + 2 * SIDE, 2 * SIDE)


def spread(local, width, z, core, aux, after=None):
    n_pair, rows, full = local.shape
    cells = SIDE * SIDE
    view = local.reshape(cells, SIDE, n_pair // (cells * SIDE), rows, full)
    blocks = []
    for step in range(SIDE):
        target = ring_target(aux * SIDE + z, core, step)
        column = lax.div(target, SIDE) * width if width < full else 0
        block = lax.dynamic_slice(
            view, (0, lax.rem(target, SIDE), 0, 0, column), (cells, 1, view.shape[2], rows, width)
        )
        if step:
            block = lax.ppermute(block, ("z", "core", "aux"), ring_pairs(step))
        blocks.append(block.reshape(2 * cells, 1, -1, rows, width))
    packed = jnp.zeros((2 * cells, SIDE, blocks[0].shape[2], rows, width), local.dtype)
    for step, block in enumerate(blocks):
        packed = lax.dynamic_update_slice(packed, block, (0, lax.rem(z + SIDE - step, SIDE), 0, 0, 0))
    if after is not None:
        packed, after = lax.optimization_barrier((packed, after))
    got = lax.all_to_all(packed, ("x", "y", "core"), split_axis=0, concat_axis=0, tiled=True)
    return got, after


def by_pair(got):
    cells = SIDE * SIDE
    _, planes, each, rows, width = got.shape
    return got.reshape(cells, 2, planes, each, rows, width).transpose(3, 0, 2, 1, 4, 5).reshape(each, -1, width)


def shards(amplitudes, ladder, cholesky, pair_ids, occ_energy, vir_energy):
    n_pair, rows, n_virt = amplitudes.shape
    half_width = n_virt // lax.axis_size("aux")
    aux, core, z = lax.axis_index("aux"), lax.axis_index("core"), lax.axis_index("z")
    x, y = lax.axis_index("x"), lax.axis_index("y")
    strip = half_width // (SIDE * SIDE)

    slot = (core * SIDE + x) * SIDE + y
    piece = lax.dynamic_slice_in_dim(cholesky, slot * strip, strip, 1)
    near = gather_plane(lax.ppermute(piece, "aux", [(0, 1), (1, 0)]))
    far = lax.ppermute(near, "core", [(0, 1), (1, 0)])

    hole = jnp.dot(
        ladder, amplitudes.reshape(n_pair, -1), preferred_element_type=jnp.float32
    ).astype(jnp.bfloat16).reshape(amplitudes.shape)
    got_amps, _ = spread(amplitudes, n_virt, z, core, aux)
    got_hole, got_amps = spread(hole, half_width, z, core, aux, got_amps)
    pair_amps = by_pair(got_amps).reshape(-1, n_virt)
    pair_hole = by_pair(got_hole)

    orbitals = jnp.arange(NO, dtype=jnp.int32)
    first_hot = (pair_ids[:, None] // NO == orbitals[None, :]).astype(jnp.float32)
    second_hot = (pair_ids[:, None] % NO == orbitals[None, :]).astype(jnp.float32)
    occ_sum = jnp.sum((first_hot + second_hot) * occ_energy[None, :], axis=1)
    vir_cols = lax.dynamic_slice_in_dim(vir_energy, aux * half_width, half_width, 0)
    place = jnp.stack([aux, core, x, y]).astype(jnp.int32)

    base = own_vectors(place, pair_amps, cholesky)
    return other_vectors(
        place, occ_sum, pair_amps, near, far, base, pair_hole, vir_energy[:, None], vir_cols[None, :]
    )


def solution(mesh):
    fine = Mesh(mesh.devices.reshape(SIDE, SIDE, SIDE, 2, 2), AXES)
    in_specs = (P(None, PAIR, None), P(), P("aux", None, None), P(PAIR), P(), P())
    out_specs = P(PAIR, None, "aux")
    return jax.shard_map(shards, mesh=fine, in_specs=in_specs, out_specs=out_specs, check_vma=False)
```

```python
import jax
import jax.numpy as jnp
from jax import lax
from jax.experimental import pallas as pl
from jax.experimental.pallas import tpu as pltpu
from jax.sharding import Mesh, PartitionSpec as P

NO = 16
AXES = ("x", "y", "z", "core", "aux")
PAIR = AXES[:4]
SIDE = 4
OWN_LIMIT = 56 * 1024 * 1024
VMEM_LIMIT = 20 * 1024 * 1024
NT = (((1,), (1,)), ((), ()))


def turned(amps_ref, cols):
    nv = cols.shape[1]
    return jnp.concatenate(
        [
            lax.dot_general(amps_ref[p * nv : (p + 1) * nv], cols, NT, preferred_element_type=jnp.float32).astype(jnp.bfloat16)
            for p in range(2)
        ],
        axis=1,
    )


def sum_vectors(nq, ready, vector, columns, amps_ref, right, total_ref, started):
    ready(0)
    right[0] = turned(amps_ref, columns(0))
    for q in range(nq):
        if q + 1 < nq:
            ready(q + 1)
            right[(q + 1) % 2] = turned(amps_ref, columns(q + 1))
        product = jnp.dot(vector(q), right[q % 2], preferred_element_type=jnp.float32)
        total_ref[...] = total_ref[...] + product if q or started else product


def split_pairs(first, second):
    rows = first.shape[1] // 2
    low = lax.broadcasted_iota(jnp.int32, first.shape, 1) < rows
    return (
        jnp.where(low, first, pltpu.roll(second, rows, axis=1)),
        jnp.where(low, pltpu.roll(first, rows, axis=1), second),
    )


def own_kernel(place_ref, got_ref, vec_ref, total_ref, amps_ref, vec, right, sems):
    nq, nv, _ = vec.shape
    half = nv // 2
    copies = [pltpu.make_async_copy(vec_ref.at[q], vec.at[q], sems.at[q]) for q in range(nq)]
    for copy in copies:
        copy.start()
    couples, _, both, _ = got_ref.shape
    chunk = couples // 8
    for i in range(8):
        tiles = [got_ref[pl.ds(i * chunk, chunk), side].astype(jnp.float32) for side in range(2)]
        for p, tile in enumerate(split_pairs(*tiles)):
            rows = chunk * both
            amps_ref[p * nv + i * rows : p * nv + (i + 1) * rows] = tile.reshape(rows, nv).astype(jnp.bfloat16)
    start = pl.multiple_of(place_ref[0] * half, half)
    sum_vectors(
        nq, lambda q: copies[q].wait(), lambda q: vec[q], lambda q: vec[q, pl.ds(start, half), :],
        amps_ref, right, total_ref, False,
    )


def estimate(nq, nv):
    return pl.CostEstimate(flops=4 * nq * nv**3, bytes_accessed=2 * nq * nv * nv, transcendentals=0)


def own_vectors(place, got, cholesky):
    nq, nv, _ = cholesky.shape
    return pl.pallas_call(
        own_kernel,
        in_specs=[
            pl.BlockSpec(memory_space=pltpu.SMEM),
            pl.BlockSpec(memory_space=pltpu.VMEM),
            pl.BlockSpec(memory_space=pltpu.HBM),
        ],
        out_specs=[pl.BlockSpec(memory_space=pltpu.VMEM)] * 2,
        out_shape=[
            jax.ShapeDtypeStruct((nv, nv), jnp.float32),
            jax.ShapeDtypeStruct((2 * nv, nv), jnp.bfloat16),
        ],
        scratch_shapes=[
            pltpu.VMEM((nq, nv, nv), jnp.bfloat16),
            pltpu.VMEM((2, nv, nv), jnp.bfloat16),
            pltpu.SemaphoreType.DMA((nq,)),
        ],
        compiler_params=pltpu.CompilerParams(vmem_limit_bytes=OWN_LIMIT),
        cost_estimate=estimate(16 * nq, nv),
        name="own_vectors",
    )(place, got, cholesky)


def other_kernel(
    place_ref, occ_ref, amps_ref, near_ref, far_ref, base_ref, hole_ref, rows_ref, cols_ref, out_ref, vec, total, right, sems
):
    nq, slots, strip, nv = vec.shape
    half, part = nv // 2, nq // 2
    core, x0, y0 = place_ref[1], place_ref[2], place_ref[3]

    fill = pltpu.make_async_copy(base_ref, total, sems.at[2])
    fill.start()
    for h in range(2):
        for owner, src in ((core, near_ref), (1 - core, far_ref)):
            for outer in range(SIDE):
                for inner in range(SIDE):
                    dx = inner + owner * (outer - inner)
                    dy = outer + owner * (inner - outer)
                    x, y = lax.rem(x0 + SIDE - dx, SIDE), lax.rem(y0 + SIDE - dy, SIDE)
                    pltpu.make_async_copy(
                        src.at[outer, inner, pl.ds(h * part, part)],
                        vec.at[pl.ds(h * part, part), (owner * SIDE + x) * SIDE + y],
                        sems.at[h],
                    ).start()
    def ready(q):
        if q % part == 0:
            block = vec.at[pl.ds(q, part)]
            pltpu.make_async_copy(block, block, sems.at[q // part]).wait()

    fill.wait()
    sum_vectors(
        nq, ready, lambda q: vec[q].reshape(nv, nv),
        lambda q: vec[q, pl.ds(place_ref[0] * (slots // 2), slots // 2)].reshape(half, nv),
        amps_ref, right, total, True,
    )
    level = rows_ref[...] + cols_ref[...]
    cells, _, planes, both, width = hole_ref.shape
    tiles = [
        hole_ref[:, side].astype(jnp.float32).reshape(cells * planes, both, width) for side in range(2)
    ]
    holes = split_pairs(*tiles)
    for p in range(out_ref.shape[0]):
        value = holes[p].reshape(nv, half) + total[:, p * half : (p + 1) * half]
        out_ref[p] = value / (level - occ_ref[p])


def other_vectors(place, occ_sum, amps, near, far, base, hole, rows, cols):
    nq, strip, nv = near.shape[2:]
    vmem = pl.BlockSpec(memory_space=pltpu.VMEM)
    smem = pl.BlockSpec(memory_space=pltpu.SMEM)
    anywhere = pl.BlockSpec(memory_space=pl.ANY)
    return pl.pallas_call(
        other_kernel,
        in_specs=[smem, smem, vmem, anywhere, anywhere, anywhere, vmem, vmem, vmem],
        out_specs=vmem,
        out_shape=jax.ShapeDtypeStruct((2, nv, nv // 2), jnp.float32),
        scratch_shapes=[
            pltpu.VMEM((nq, nv // strip, strip, nv), jnp.bfloat16),
            pltpu.VMEM((nv, nv), jnp.float32),
            pltpu.VMEM((2, nv, nv), jnp.bfloat16),
            pltpu.SemaphoreType.DMA((3,)),
        ],
        compiler_params=pltpu.CompilerParams(vmem_limit_bytes=VMEM_LIMIT),
        cost_estimate=estimate(nq, nv),
        name="other_vectors",
    )(place, occ_sum, amps, near, far, base, hole, rows, cols)


def plane_shift(block, shift, first_core_axis):
    pairs = []
    for x in range(SIDE):
        for y in range(SIDE):
            for core in range(2):
                if core == first_core_axis:
                    to = x * SIDE + (y + shift) % SIDE
                else:
                    to = (x + shift) % SIDE * SIDE + y
                pairs.append(((x * SIDE + y) * 2 + core, to * 2 + core))
    return lax.ppermute(block, ("x", "y", "core"), pairs)


def gather_plane(block):
    for stage in range(2):
        block = jnp.stack([block] + [plane_shift(block, d, 1 - stage) for d in (1, 2, 3)])
    return block


def ring_pairs(step):
    steps = {1: (1, 1), 3: (-1, -1), 2: (2, -2)}[step]
    pairs = []
    for z8 in range(2 * SIDE):
        for core in range(2):
            to = (z8 + steps[core]) % (2 * SIDE)
            pairs.append(((z8 % SIDE * 2 + core) * 2 + z8 // SIDE, (to % SIDE * 2 + core) * 2 + to // SIDE))
    return pairs


def ring_target(z8, core, step):
    move = {0: 0, 1: 1, 3: -1}.get(step)
    move = 2 - 4 * core if move is None else move
    return lax.rem(z8 + move + 2 * SIDE, 2 * SIDE)


def spread(hole, width, z, core, aux, after):
    n_pair, rows, full = hole.shape
    cells, each = SIDE * SIDE, n_pair // (2 * SIDE**3)
    view = hole.reshape(cells, SIDE, 2, each * rows, full)
    packed = jnp.zeros((2 * cells, SIDE, each * rows, width), hole.dtype)
    for step in range(SIDE):
        target = ring_target(aux * SIDE + z, core, step)
        column = lax.div(target, SIDE) * width
        block = lax.dynamic_slice(
            view, (0, lax.rem(target, SIDE), 0, 0, column), (cells, 1, 2, each * rows, width)
        )
        if step:
            block = lax.ppermute(block, ("z", "core", "aux"), ring_pairs(step))
        block = block.reshape(2 * cells, 1, each * rows, width)
        packed = lax.dynamic_update_slice(packed, block, (0, lax.rem(z + SIDE - step, SIDE), 0, 0))
    packed, after = lax.optimization_barrier((packed, after))
    got = lax.all_to_all(packed, ("x", "y", "core"), split_axis=0, concat_axis=0, tiled=True)
    return got.reshape(cells, 2, SIDE, each * rows, width), after


def shards(amplitudes, ladder, cholesky, pair_ids, occ_energy, vir_energy):
    n_pair, rows, n_virt = amplitudes.shape
    half_width = n_virt // lax.axis_size("aux")
    aux, core, z = lax.axis_index("aux"), lax.axis_index("core"), lax.axis_index("z")
    x, y = lax.axis_index("x"), lax.axis_index("y")
    strip = half_width // (SIDE * SIDE)

    slot = (core * SIDE + x) * SIDE + y
    piece = lax.dynamic_slice_in_dim(cholesky, slot * strip, strip, 1)
    piece = lax.ppermute(piece, "aux", [(0, 1), (1, 0)])
    hole = jnp.dot(
        ladder, amplitudes.reshape(n_pair, -1), preferred_element_type=jnp.float32
    ).astype(jnp.bfloat16).reshape(amplitudes.shape)
    packed = amplitudes.reshape(n_pair // 2, 2 * rows, n_virt)
    packed, piece, hole = lax.optimization_barrier((packed, piece, hole))
    near = gather_plane(piece)
    far = lax.ppermute(near, "core", [(0, 1), (1, 0)])

    got_amps = lax.all_to_all(packed, PAIR, split_axis=0, concat_axis=0, tiled=True)
    pair_hole, got_amps = spread(hole, half_width, z, core, aux, got_amps)
    got_amps = got_amps.reshape(n_pair // 4, 2, 2 * rows, n_virt)

    orbitals = jnp.arange(NO, dtype=jnp.int32)
    first_hot = (pair_ids[:, None] // NO == orbitals[None, :]).astype(jnp.float32)
    second_hot = (pair_ids[:, None] % NO == orbitals[None, :]).astype(jnp.float32)
    occ_sum = jnp.sum((first_hot + second_hot) * occ_energy[None, :], axis=1)
    vir_cols = lax.dynamic_slice_in_dim(vir_energy, aux * half_width, half_width, 0)
    place = jnp.stack([aux, core, x, y]).astype(jnp.int32)

    base, pair_amps = own_vectors(place, got_amps, cholesky)
    return other_vectors(
        place, occ_sum, pair_amps, near, far, base, pair_hole, vir_energy[:, None], vir_cols[None, :]
    )


def solution(mesh):
    fine = Mesh(mesh.devices.reshape(SIDE, SIDE, SIDE, 2, 2), AXES)
    in_specs = (P(None, PAIR, None), P(), P("aux", None, None), P(PAIR), P(), P())
    out_specs = P(PAIR, None, "aux")
    return jax.shard_map(shards, mesh=fine, in_specs=in_specs, out_specs=out_specs, check_vma=False)
```

```python
import jax
import jax.numpy as jnp
from jax import lax
from jax.experimental import pallas as pl
from jax.experimental.pallas import tpu as pltpu
from jax.sharding import Mesh, PartitionSpec as P

NO = 16
AXES = ("x", "y", "z", "core", "aux")
PAIR = AXES[:4]
SIDE = 4
VMEM_LIMIT = 56 * 1024 * 1024
NT = (((1,), (1,)), ((), ()))


def turned(amps_ref, cols):
    nv = cols.shape[1]
    return jnp.concatenate(
        [
            lax.dot_general(amps_ref[p * nv : (p + 1) * nv], cols, NT, preferred_element_type=jnp.float32).astype(jnp.bfloat16)
            for p in range(2)
        ],
        axis=1,
    )


def split_pairs(first, second):
    rows = first.shape[1] // 2
    low = lax.broadcasted_iota(jnp.int32, first.shape, 1) < rows
    return (
        jnp.where(low, first, pltpu.roll(second, rows, axis=1)),
        jnp.where(low, pltpu.roll(first, rows, axis=1), second),
    )


def particle_kernel(
    place_ref, occ_ref, got_hbm, own_hbm, near_hbm, far_hbm, rows_ref, cols_ref, out_hbm,
    got_ref, amps_ref, own, other, right, total, out_ref, sems,
):
    nq, nv, _ = own.shape
    half, part = nv // 2, nq // 2
    slots = other.shape[1]
    aux, core, x0, y0 = (place_ref[i] for i in range(4))

    fetch = pltpu.make_async_copy(got_hbm, got_ref, sems.at[nq])
    fetch.start()
    own_copies = [pltpu.make_async_copy(own_hbm.at[q], own.at[q], sems.at[q]) for q in range(nq)]
    for copy in own_copies:
        copy.start()
    for h in range(2):
        for owner, src in ((core, near_hbm), (1 - core, far_hbm)):
            for outer in range(SIDE):
                for inner in range(SIDE):
                    dx = inner + owner * (outer - inner)
                    dy = outer + owner * (inner - outer)
                    x, y = lax.rem(x0 + SIDE - dx, SIDE), lax.rem(y0 + SIDE - dy, SIDE)
                    pltpu.make_async_copy(
                        src.at[outer, inner, pl.ds(h * part, part)],
                        other.at[pl.ds(h * part, part), (owner * SIDE + x) * SIDE + y],
                        sems.at[nq + 1 + h],
                    ).start()
    fetch.wait()

    couples, _, both, _ = got_ref.shape
    chunk = couples // 8
    for i in range(8):
        tiles = [got_ref[pl.ds(i * chunk, chunk), side, :, :nv].astype(jnp.float32) for side in range(2)]
        for p, tile in enumerate(split_pairs(*tiles)):
            rows = chunk * both
            amps_ref[p * nv + i * rows : p * nv + (i + 1) * rows] = tile.reshape(rows, nv).astype(jnp.bfloat16)

    def ready(q):
        if q < nq:
            own_copies[q].wait()
        elif (q - nq) % part == 0:
            block = other.at[pl.ds(q - nq, part)]
            pltpu.make_async_copy(block, block, sems.at[nq + 1 + (q - nq) // part]).wait()

    def columns(q):
        if q < nq:
            return own[q, pl.ds(pl.multiple_of(aux * half, half), half), :]
        return other[q - nq, pl.ds(aux * (slots // 2), slots // 2)].reshape(half, nv)

    def vector(q):
        return own[q] if q < nq else other[q - nq].reshape(nv, nv)

    ready(0)
    right[0] = turned(amps_ref, columns(0))
    for q in range(2 * nq):
        if q + 1 < 2 * nq:
            ready(q + 1)
            right[(q + 1) % 2] = turned(amps_ref, columns(q + 1))
        product = jnp.dot(vector(q), right[q % 2], preferred_element_type=jnp.float32)
        total[...] = total[...] + product if q else product

    level = rows_ref[...] + cols_ref[...]
    tiles = [got_ref[:, side, :, nv:].astype(jnp.float32) for side in range(2)]
    stores = []
    for p, hole in enumerate(split_pairs(*tiles)):
        value = hole.reshape(nv, half) + total[:, p * half : (p + 1) * half]
        out_ref[p] = value / (level - occ_ref[p])
        stores.append(pltpu.make_async_copy(out_ref.at[p], out_hbm.at[p], sems.at[p]))
        stores[p].start()
    for store in stores:
        store.wait()


def particle(place, occ_sum, got, own, near, far, rows, cols):
    nq, nv, _ = own.shape
    slots = nv // near.shape[3]
    vmem = pl.BlockSpec(memory_space=pltpu.VMEM)
    smem = pl.BlockSpec(memory_space=pltpu.SMEM)
    anywhere = pl.BlockSpec(memory_space=pl.ANY)
    return pl.pallas_call(
        particle_kernel,
        in_specs=[smem, smem, anywhere, anywhere, anywhere, anywhere, vmem, vmem],
        out_specs=anywhere,
        out_shape=jax.ShapeDtypeStruct((2, nv, nv // 2), jnp.float32),
        scratch_shapes=[
            pltpu.VMEM(got.shape, jnp.bfloat16),
            pltpu.VMEM((2 * nv, nv), jnp.bfloat16),
            pltpu.VMEM((nq, nv, nv), jnp.bfloat16),
            pltpu.VMEM((nq, slots, nv // slots, nv), jnp.bfloat16),
            pltpu.VMEM((2, nv, nv), jnp.bfloat16),
            pltpu.VMEM((nv, nv), jnp.float32),
            pltpu.VMEM((2, nv, nv // 2), jnp.float32),
            pltpu.SemaphoreType.DMA((nq + 3,)),
        ],
        compiler_params=pltpu.CompilerParams(vmem_limit_bytes=VMEM_LIMIT),
        cost_estimate=pl.CostEstimate(
            flops=8 * nq * nv**3, bytes_accessed=4 * nq * nv * nv, transcendentals=0
        ),
        name="particle",
    )(place, occ_sum, got, own, near, far, rows, cols)


def plane_shift(block, shift, first_core_axis):
    pairs = []
    for x in range(SIDE):
        for y in range(SIDE):
            for core in range(2):
                if core == first_core_axis:
                    to = x * SIDE + (y + shift) % SIDE
                else:
                    to = (x + shift) % SIDE * SIDE + y
                pairs.append(((x * SIDE + y) * 2 + core, to * 2 + core))
    return lax.ppermute(block, ("x", "y", "core"), pairs)


def gather_plane(block):
    for stage in range(2):
        block = jnp.stack([block] + [plane_shift(block, d, 1 - stage) for d in (1, 2, 3)])
    return block


def shards(amplitudes, ladder, cholesky, pair_ids, occ_energy, vir_energy):
    n_pair, rows, n_virt = amplitudes.shape
    half_width = n_virt // lax.axis_size("aux")
    aux, core = lax.axis_index("aux"), lax.axis_index("core")
    x, y = lax.axis_index("x"), lax.axis_index("y")
    strip = half_width // (SIDE * SIDE)

    slot = (core * SIDE + x) * SIDE + y
    piece = lax.dynamic_slice_in_dim(cholesky, slot * strip, strip, 1)
    piece = lax.ppermute(piece, "aux", [(0, 1), (1, 0)])

    mine = lax.dynamic_slice_in_dim(amplitudes, aux * half_width, half_width, 2)
    hole = jnp.dot(
        ladder, mine.reshape(n_pair, -1), preferred_element_type=jnp.float32
    ).astype(jnp.bfloat16)
    packed = jnp.concatenate(
        [amplitudes.reshape(-1, 2 * rows, n_virt), hole.reshape(-1, 2 * rows, half_width)], axis=2
    )
    packed, piece = lax.optimization_barrier((packed, piece))
    got = lax.all_to_all(packed, PAIR, split_axis=0, concat_axis=0, tiled=True)
    got = got.reshape(-1, 2, *got.shape[1:])
    near = gather_plane(piece)
    far = lax.ppermute(near, "core", [(0, 1), (1, 0)])

    orbitals = jnp.arange(NO, dtype=jnp.int32)
    first_hot = (pair_ids[:, None] // NO == orbitals[None, :]).astype(jnp.float32)
    second_hot = (pair_ids[:, None] % NO == orbitals[None, :]).astype(jnp.float32)
    occ_sum = jnp.sum((first_hot + second_hot) * occ_energy[None, :], axis=1)
    vir_cols = lax.dynamic_slice_in_dim(vir_energy, aux * half_width, half_width, 0)
    place = jnp.stack([aux, core, x, y]).astype(jnp.int32)

    return particle(place, occ_sum, got, cholesky, near, far, vir_energy[:, None], vir_cols[None, :])


def solution(mesh):
    fine = Mesh(mesh.devices.reshape(SIDE, SIDE, SIDE, 2, 2), AXES)
    in_specs = (P(None, PAIR, None), P(), P("aux", None, None), P(PAIR), P(), P())
    out_specs = P(PAIR, None, "aux")
    return jax.shard_map(shards, mesh=fine, in_specs=in_specs, out_specs=out_specs, check_vma=False)
```

```python
import jax
import jax.numpy as jnp
from jax import lax
from jax.experimental import pallas as pl
from jax.experimental.pallas import tpu as pltpu
from jax.sharding import Mesh, PartitionSpec as P

NO = 16
AXES = ("x", "y", "z", "core", "aux")
PAIR = AXES[:4]
SIDE = 4
VMEM_LIMIT = 56 * 1024 * 1024
WEIGHT = 20 * 10**9
NT = (((1,), (1,)), ((), ()))


def turned(amps_ref, cols):
    nv = cols.shape[1]
    return jnp.concatenate(
        [
            lax.dot_general(amps_ref[p * nv : (p + 1) * nv], cols, NT, preferred_element_type=jnp.float32).astype(jnp.bfloat16)
            for p in range(2)
        ],
        axis=1,
    )


def split_pairs(first, second):
    rows = first.shape[1] // 2
    low = lax.broadcasted_iota(jnp.int32, first.shape, 1) < rows
    return (
        jnp.where(low, first, pltpu.roll(second, rows, axis=1)),
        jnp.where(low, pltpu.roll(first, rows, axis=1), second),
    )


def particle_kernel(
    place_ref, occ_ref, got_hbm, one_hbm, two_hbm, three_hbm, own_hbm, near_hbm, far_hbm, rows_ref, cols_ref, out_hbm,
    got_ref, amps_ref, own, other, right, total, out_ref, sems,
):
    nq, nv, _ = own.shape
    half, part = nv // 2, nq // 2
    slots = other.shape[1]
    aux, core, x0, y0, z = (place_ref[i] for i in range(5))

    fetches = []
    for step, src in enumerate((got_hbm.at[:, :, z], one_hbm, two_hbm, three_hbm)):
        fetches.append(pltpu.make_async_copy(src, got_ref.at[:, lax.rem(z + SIDE - step, SIDE)], sems.at[nq + 3 + step]))
        fetches[step].start()
    own_copies = [pltpu.make_async_copy(own_hbm.at[q], own.at[q], sems.at[q]) for q in range(nq)]
    for copy in own_copies:
        copy.start()
    for h in range(2):
        for owner, src in ((core, near_hbm), (1 - core, far_hbm)):
            for outer in range(SIDE):
                for inner in range(SIDE):
                    dx = inner + owner * (outer - inner)
                    dy = outer + owner * (inner - outer)
                    x, y = lax.rem(x0 + SIDE - dx, SIDE), lax.rem(y0 + SIDE - dy, SIDE)
                    pltpu.make_async_copy(
                        src.at[outer, inner, pl.ds(h * part, part)],
                        other.at[pl.ds(h * part, part), (owner * SIDE + x) * SIDE + y],
                        sems.at[nq + 1 + h],
                    ).start()
    for fetch in fetches:
        fetch.wait()

    cells, planes, _, both, _ = got_ref.shape
    chunk = cells * planes // 8

    def tiles_of(begin, count, lanes):
        return [
            got_ref[begin : begin + count, :, side, :, lanes].astype(jnp.float32).reshape(count * planes, both, -1)
            for side in range(2)
        ]

    for i in range(8):
        tiles = tiles_of(i * (cells // 8), cells // 8, slice(0, nv))
        for p, tile in enumerate(split_pairs(*tiles)):
            rows = chunk * both
            amps_ref[p * nv + i * rows : p * nv + (i + 1) * rows] = tile.reshape(rows, nv).astype(jnp.bfloat16)

    def ready(q):
        if q < nq:
            own_copies[q].wait()
        elif (q - nq) % part == 0:
            block = other.at[pl.ds(q - nq, part)]
            pltpu.make_async_copy(block, block, sems.at[nq + 1 + (q - nq) // part]).wait()

    def columns(q):
        if q < nq:
            return own[q, pl.ds(pl.multiple_of(aux * half, half), half), :]
        return other[q - nq, pl.ds(aux * (slots // 2), slots // 2)].reshape(half, nv)

    def vector(q):
        return own[q] if q < nq else other[q - nq].reshape(nv, nv)

    ready(0)
    right[0] = turned(amps_ref, columns(0))
    for q in range(2 * nq):
        if q + 1 < 2 * nq:
            ready(q + 1)
            right[(q + 1) % 2] = turned(amps_ref, columns(q + 1))
        product = jnp.dot(vector(q), right[q % 2], preferred_element_type=jnp.float32)
        total[...] = total[...] + product if q else product

    level = rows_ref[...] + cols_ref[...]
    tiles = tiles_of(0, cells, slice(nv, nv + half))
    stores = []
    for p, hole in enumerate(split_pairs(*tiles)):
        value = hole.reshape(nv, half) + total[:, p * half : (p + 1) * half]
        out_ref[p] = value / (level - occ_ref[p])
        stores.append(pltpu.make_async_copy(out_ref.at[p], out_hbm.at[p], sems.at[p]))
        stores[p].start()
    for store in stores:
        store.wait()


def particle(place, occ_sum, got, ring, own, near, far, rows, cols):
    nq, nv, _ = own.shape
    slots = nv // near.shape[3]
    vmem = pl.BlockSpec(memory_space=pltpu.VMEM)
    smem = pl.BlockSpec(memory_space=pltpu.SMEM)
    anywhere = pl.BlockSpec(memory_space=pl.ANY)
    return pl.pallas_call(
        particle_kernel,
        in_specs=[smem, smem, *[anywhere] * 7, vmem, vmem],
        out_specs=anywhere,
        out_shape=jax.ShapeDtypeStruct((2, nv, nv // 2), jnp.float32),
        scratch_shapes=[
            pltpu.VMEM((got.shape[0], SIDE, 2, *got.shape[3:]), jnp.bfloat16),
            pltpu.VMEM((2 * nv, nv), jnp.bfloat16),
            pltpu.VMEM((nq, nv, nv), jnp.bfloat16),
            pltpu.VMEM((nq, slots, nv // slots, nv), jnp.bfloat16),
            pltpu.VMEM((2, nv, nv), jnp.bfloat16),
            pltpu.VMEM((nv, nv), jnp.float32),
            pltpu.VMEM((2, nv, nv // 2), jnp.float32),
            pltpu.SemaphoreType.DMA((nq + 3 + SIDE,)),
        ],
        compiler_params=pltpu.CompilerParams(vmem_limit_bytes=VMEM_LIMIT),
        cost_estimate=pl.CostEstimate(
            flops=8 * nq * nv**3, bytes_accessed=4 * nq * nv * nv, transcendentals=0
        ),
        name="particle",
    )(place, occ_sum, got, *ring, own, near, far, rows, cols)


def arrived_kernel(place_ref, *refs):
    for i in range(place_ref.shape[0]):
        refs[-1][i] = place_ref[i]


def arrived(place, ring):
    smem = pl.BlockSpec(memory_space=pltpu.SMEM)
    return pl.pallas_call(
        arrived_kernel,
        in_specs=[smem, *[pl.BlockSpec(memory_space=pl.ANY)] * len(ring)],
        out_specs=smem,
        out_shape=jax.ShapeDtypeStruct(place.shape, place.dtype),
        cost_estimate=pl.CostEstimate(flops=WEIGHT, bytes_accessed=0, transcendentals=0),
        name="arrived",
    )(place, *ring)


def plane_shift(block, shift, first_core_axis):
    pairs = []
    for x in range(SIDE):
        for y in range(SIDE):
            for core in range(2):
                if core == first_core_axis:
                    to = x * SIDE + (y + shift) % SIDE
                else:
                    to = (x + shift) % SIDE * SIDE + y
                pairs.append(((x * SIDE + y) * 2 + core, to * 2 + core))
    return lax.ppermute(block, ("x", "y", "core"), pairs)


def gather_plane(block):
    for stage in range(2):
        block = jnp.stack([block] + [plane_shift(block, d, 1 - stage) for d in (1, 2, 3)])
    return block


def ring_pairs(step):
    steps = {1: (1, 1), 3: (-1, -1), 2: (2, -2)}[step]
    pairs = []
    for z8 in range(2 * SIDE):
        for core in range(2):
            to = (z8 + steps[core]) % (2 * SIDE)
            pairs.append(((z8 % SIDE * 2 + core) * 2 + z8 // SIDE, (to % SIDE * 2 + core) * 2 + to // SIDE))
    return pairs


def shards(amplitudes, ladder, cholesky, pair_ids, occ_energy, vir_energy):
    n_pair, rows, n_virt = amplitudes.shape
    half_width = n_virt // lax.axis_size("aux")
    aux, core = lax.axis_index("aux"), lax.axis_index("core")
    x, y, z = lax.axis_index("x"), lax.axis_index("y"), lax.axis_index("z")
    strip = half_width // (SIDE * SIDE)

    slot = (core * SIDE + x) * SIDE + y
    piece = lax.dynamic_slice_in_dim(cholesky, slot * strip, strip, 1)
    piece = lax.ppermute(piece, "aux", [(0, 1), (1, 0)])

    hole = jnp.dot(
        ladder, amplitudes.reshape(n_pair, -1), preferred_element_type=jnp.float32
    ).astype(jnp.bfloat16)
    blocks = (SIDE * SIDE, SIDE, 2, 2 * rows)
    hole = hole.reshape(*blocks, n_virt)
    step = lax.rem(jnp.arange(SIDE) - z + SIDE, SIDE)[:, None]
    move = jnp.where(step == 3, -1, jnp.where(step == 2, 2 - 4 * jnp.arange(2)[None, :], step))
    upper = lax.rem(aux * SIDE + z + move + 2 * SIDE, 2 * SIDE) >= SIDE
    hole = jnp.where(upper[None, :, :, None, None], hole[..., half_width:], hole[..., :half_width])
    packed = jnp.concatenate([amplitudes.reshape(*blocks, n_virt), hole], axis=4)
    packed = packed.transpose(0, 2, 1, 3, 4).reshape(2 * SIDE * SIDE, SIDE, 2 * rows, -1)
    packed, piece = lax.optimization_barrier((packed, piece))
    got = lax.all_to_all(packed, ("x", "y", "core"), split_axis=0, concat_axis=0, tiled=True)
    ring = []
    for d in range(1, SIDE):
        block = lax.dynamic_slice_in_dim(got, lax.rem(z + d, SIDE), 1, 1)
        block = lax.ppermute(block, ("z", "core", "aux"), ring_pairs(d))
        ring.append(block.reshape(SIDE * SIDE, 2, 2 * rows, -1))
    got = got.reshape(SIDE * SIDE, 2, SIDE, 2 * rows, -1)
    near = gather_plane(piece)
    far = lax.ppermute(near, "core", [(0, 1), (1, 0)])

    orbitals = jnp.arange(NO, dtype=jnp.int32)
    first_hot = (pair_ids[:, None] // NO == orbitals[None, :]).astype(jnp.float32)
    second_hot = (pair_ids[:, None] % NO == orbitals[None, :]).astype(jnp.float32)
    occ_sum = jnp.sum((first_hot + second_hot) * occ_energy[None, :], axis=1)
    vir_cols = lax.dynamic_slice_in_dim(vir_energy, aux * half_width, half_width, 0)
    place = jnp.stack([aux, core, x, y, z]).astype(jnp.int32)

    return particle(arrived(place, ring), occ_sum, got, ring, cholesky, near, far, vir_energy[:, None], vir_cols[None, :])


def solution(mesh):
    fine = Mesh(mesh.devices.reshape(SIDE, SIDE, SIDE, 2, 2), AXES)
    in_specs = (P(None, PAIR, None), P(), P("aux", None, None), P(PAIR), P(), P())
    out_specs = P(PAIR, None, "aux")
    return jax.shard_map(shards, mesh=fine, in_specs=in_specs, out_specs=out_specs, check_vma=False)
```

```python
import jax
import jax.numpy as jnp
from jax import lax
from jax.experimental import pallas as pl
from jax.experimental.pallas import tpu as pltpu
from jax.sharding import Mesh, PartitionSpec as P

NO = 16
AXES = ("x", "y", "z", "core", "aux")
PAIR = AXES[:4]
SIDE = 4
OWN_LIMIT = 48 * 1024 * 1024
OTHER_LIMIT = 48 * 1024 * 1024
WEIGHT = 4
NT = (((1,), (1,)), ((), ()))


def turned(amps_ref, cols):
    nv = cols.shape[1]
    return jnp.concatenate(
        [
            lax.dot_general(amps_ref[p * nv : (p + 1) * nv], cols, NT, preferred_element_type=jnp.float32).astype(jnp.bfloat16)
            for p in range(2)
        ],
        axis=1,
    )


def split_pairs(first, second):
    rows = first.shape[1] // 2
    low = lax.broadcasted_iota(jnp.int32, first.shape, 1) < rows
    return (
        jnp.where(low, first, pltpu.roll(second, rows, axis=1)),
        jnp.where(low, pltpu.roll(first, rows, axis=1), second),
    )


def add_vectors(nq, ready, vector, columns, amps_ref, right, total, started):
    ready(0)
    right[0] = turned(amps_ref, columns(0))
    for q in range(nq):
        if q + 1 < nq:
            ready(q + 1)
            right[(q + 1) % 2] = turned(amps_ref, columns(q + 1))
        product = jnp.dot(vector(q), right[q % 2], preferred_element_type=jnp.float32)
        total[...] = total[...] + product if q or started else product


def own_kernel(place_ref, got_hbm, own_hbm, total, amps_ref, got_ref, own, right, sems):
    nq, nv, _ = own.shape
    half = nv // 2
    fetch = pltpu.make_async_copy(got_hbm.at[:, :, :, pl.ds(0, nv)], got_ref, sems.at[nq])
    fetch.start()
    copies = [pltpu.make_async_copy(own_hbm.at[q], own.at[q], sems.at[q]) for q in range(nq)]
    for copy in copies:
        copy.start()
    fetch.wait()
    couples, _, both, _ = got_ref.shape
    chunk = couples // 8
    for i in range(8):
        tiles = [got_ref[pl.ds(i * chunk, chunk), side].astype(jnp.float32) for side in range(2)]
        for p, tile in enumerate(split_pairs(*tiles)):
            rows = chunk * both
            amps_ref[p * nv + i * rows : p * nv + (i + 1) * rows] = tile.reshape(rows, nv).astype(jnp.bfloat16)
    start = pl.multiple_of(place_ref[0] * half, half)
    add_vectors(
        nq, lambda q: copies[q].wait(), lambda q: own[q], lambda q: own[q, pl.ds(start, half), :],
        amps_ref, right, total, False,
    )


def other_kernel(*refs):
    place_ref, occ_ref, got_hbm, base_hbm, amps_hbm = refs[:5]
    sources, (rows_ref, cols_ref, out_hbm) = refs[5 : 5 + 2 * SIDE], refs[5 + 2 * SIDE : 8 + 2 * SIDE]
    got_ref, amps_ref, other, right, total, out_ref, sems = refs[8 + 2 * SIDE :]
    nq, slots, _, nv = other.shape
    half, part = nv // 2, nq // 2
    aux, core, x0, y0 = (place_ref[i] for i in range(4))
    load = pltpu.make_async_copy(amps_hbm, amps_ref, sems.at[6])
    load.start()
    for h in range(2):
        for owner, blocks in ((core, sources[:SIDE]), (1 - core, sources[SIDE:])):
            for outer, src in enumerate(blocks):
                for inner in range(SIDE):
                    dx = inner + owner * (outer - inner)
                    dy = outer + owner * (inner - outer)
                    x, y = lax.rem(x0 + SIDE - dx, SIDE), lax.rem(y0 + SIDE - dy, SIDE)
                    pltpu.make_async_copy(
                        src.at[inner, pl.ds(h * part, part)],
                        other.at[pl.ds(h * part, part), (owner * SIDE + x) * SIDE + y],
                        sems.at[h],
                    ).start()
    fill = pltpu.make_async_copy(base_hbm, total, sems.at[2])
    fill.start()
    fetch = pltpu.make_async_copy(got_hbm.at[:, :, :, pl.ds(nv, half)], got_ref, sems.at[3])
    fetch.start()

    def ready(q):
        if q % part == 0:
            block = other.at[pl.ds(q, part)]
            pltpu.make_async_copy(block, block, sems.at[q // part]).wait()

    fill.wait()
    load.wait()
    add_vectors(
        nq, ready, lambda q: other[q].reshape(nv, nv),
        lambda q: other[q, pl.ds(aux * (slots // 2), slots // 2)].reshape(half, nv),
        amps_ref, right, total, True,
    )
    fetch.wait()
    level = rows_ref[...] + cols_ref[...]
    tiles = [got_ref[:, side].astype(jnp.float32) for side in range(2)]
    stores = []
    for p, hole in enumerate(split_pairs(*tiles)):
        value = hole.reshape(nv, half) + total[:, p * half : (p + 1) * half]
        out_ref[p] = value / (level - occ_ref[p])
        stores.append(pltpu.make_async_copy(out_ref.at[p], out_hbm.at[p], sems.at[4 + p]))
        stores[p].start()
    for store in stores:
        store.wait()


def estimate(nq, nv):
    return pl.CostEstimate(flops=4 * nq * nv**3, bytes_accessed=2 * nq * nv * nv, transcendentals=0)


VMEM = pl.BlockSpec(memory_space=pltpu.VMEM)
SMEM = pl.BlockSpec(memory_space=pltpu.SMEM)
ANYWHERE = pl.BlockSpec(memory_space=pl.ANY)


def own_vectors(place, got, own):
    nq, nv, _ = own.shape
    return pl.pallas_call(
        own_kernel,
        in_specs=[SMEM, ANYWHERE, ANYWHERE],
        out_specs=[VMEM, VMEM],
        out_shape=[
            jax.ShapeDtypeStruct((nv, nv), jnp.float32),
            jax.ShapeDtypeStruct((2 * nv, nv), jnp.bfloat16),
        ],
        scratch_shapes=[
            pltpu.VMEM((*got.shape[:3], nv), jnp.bfloat16),
            pltpu.VMEM((nq, nv, nv), jnp.bfloat16),
            pltpu.VMEM((2, nv, nv), jnp.bfloat16),
            pltpu.SemaphoreType.DMA((nq + 1,)),
        ],
        compiler_params=pltpu.CompilerParams(vmem_limit_bytes=OWN_LIMIT),
        cost_estimate=estimate(WEIGHT * nq, nv),
        name="own_vectors",
    )(place, got, own)


def other_vectors(place, occ_sum, got, base, amps, near, far, rows, cols):
    nq, strip, nv = near[0].shape[1:]
    return pl.pallas_call(
        other_kernel,
        in_specs=[SMEM, SMEM, *[ANYWHERE] * (3 + 2 * SIDE), VMEM, VMEM],
        out_specs=ANYWHERE,
        out_shape=jax.ShapeDtypeStruct((2, nv, nv // 2), jnp.float32),
        scratch_shapes=[
            pltpu.VMEM((*got.shape[:3], nv // 2), jnp.bfloat16),
            pltpu.VMEM(amps.shape, jnp.bfloat16),
            pltpu.VMEM((nq, nv // strip, strip, nv), jnp.bfloat16),
            pltpu.VMEM((2, nv, nv), jnp.bfloat16),
            pltpu.VMEM((nv, nv), jnp.float32),
            pltpu.VMEM((2, nv, nv // 2), jnp.float32),
            pltpu.SemaphoreType.DMA((7,)),
        ],
        compiler_params=pltpu.CompilerParams(vmem_limit_bytes=OTHER_LIMIT),
        cost_estimate=estimate(nq, nv),
        name="other_vectors",
    )(place, occ_sum, got, base, amps, *near, *far, rows, cols)


def plane_shift(block, shift, first_core_axis):
    pairs = []
    for x in range(SIDE):
        for y in range(SIDE):
            for core in range(2):
                if core == first_core_axis:
                    to = x * SIDE + (y + shift) % SIDE
                else:
                    to = (x + shift) % SIDE * SIDE + y
                pairs.append(((x * SIDE + y) * 2 + core, to * 2 + core))
    return lax.ppermute(block, ("x", "y", "core"), pairs)


def gather_plane(block):
    shifts = range(1, SIDE)
    block = jnp.stack([block] + [plane_shift(block, d, 1) for d in shifts])
    return [block] + [plane_shift(block, d, 0) for d in shifts]


def other_core(block):
    return lax.ppermute(block, "core", [(0, 1), (1, 0)])


def shards(amplitudes, ladder, cholesky, pair_ids, occ_energy, vir_energy):
    n_pair, rows, n_virt = amplitudes.shape
    half_width = n_virt // lax.axis_size("aux")
    aux, core = lax.axis_index("aux"), lax.axis_index("core")
    x, y = lax.axis_index("x"), lax.axis_index("y")
    strip = half_width // (SIDE * SIDE)

    slot = (core * SIDE + x) * SIDE + y
    piece = lax.dynamic_slice_in_dim(cholesky, slot * strip, strip, 1)
    piece = lax.ppermute(piece, "aux", [(0, 1), (1, 0)])

    mine = lax.dynamic_slice_in_dim(amplitudes, aux * half_width, half_width, 2)
    hole = jnp.dot(
        ladder, mine.reshape(n_pair, -1), preferred_element_type=jnp.float32
    ).astype(jnp.bfloat16)
    packed = jnp.concatenate(
        [amplitudes.reshape(-1, 2 * rows, n_virt), hole.reshape(-1, 2 * rows, half_width)], axis=2
    )
    packed, piece = lax.optimization_barrier((packed, piece))
    got = lax.all_to_all(packed, PAIR, split_axis=0, concat_axis=0, tiled=True)
    got = got.reshape(-1, 2, *got.shape[1:])
    near = gather_plane(piece)

    orbitals = jnp.arange(NO, dtype=jnp.int32)
    first_hot = (pair_ids[:, None] // NO == orbitals[None, :]).astype(jnp.float32)
    second_hot = (pair_ids[:, None] % NO == orbitals[None, :]).astype(jnp.float32)
    occ_sum = jnp.sum((first_hot + second_hot) * occ_energy[None, :], axis=1)
    vir_cols = lax.dynamic_slice_in_dim(vir_energy, aux * half_width, half_width, 0)
    place = jnp.stack([aux, core, x, y]).astype(jnp.int32)

    base, pair_amps = own_vectors(place, got, cholesky)
    *late, base = lax.optimization_barrier((*near[1:], base))
    near = [near[0], *late]
    far = [other_core(block) for block in near]
    return other_vectors(
        place, occ_sum, got, base, pair_amps, near, far, vir_energy[:, None], vir_cols[None, :]
    )


def solution(mesh):
    fine = Mesh(mesh.devices.reshape(SIDE, SIDE, SIDE, 2, 2), AXES)
    in_specs = (P(None, PAIR, None), P(), P("aux", None, None), P(PAIR), P(), P())
    out_specs = P(PAIR, None, "aux")
    return jax.shard_map(shards, mesh=fine, in_specs=in_specs, out_specs=out_specs, check_vma=False)
```

```python
import jax
import jax.numpy as jnp
from jax import lax
from jax.experimental import pallas as pl
from jax.experimental.pallas import tpu as pltpu
from jax.sharding import Mesh, PartitionSpec as P

NO = 16
AXES = ("x", "y", "z", "core", "aux")
PAIR = AXES[:4]
SIDE = 4
VMEM_LIMIT = 56 * 1024 * 1024
NT = (((1,), (1,)), ((), ()))


def turned(amps_ref, cols):
    nv = cols.shape[1]
    return jnp.concatenate(
        [
            lax.dot_general(amps_ref[p * nv : (p + 1) * nv], cols, NT, preferred_element_type=jnp.float32).astype(jnp.bfloat16)
            for p in range(2)
        ],
        axis=1,
    )


def split_pairs(first, second):
    rows = first.shape[1] // 2
    low = lax.broadcasted_iota(jnp.int32, first.shape, 1) < rows
    return (
        jnp.where(low, first, pltpu.roll(second, rows, axis=1)),
        jnp.where(low, pltpu.roll(first, rows, axis=1), second),
    )


def particle_kernel(
    place_ref, occ_ref, got_hbm, own_hbm, near_hbm, far_hbm, rows_ref, cols_ref, out_hbm,
    got_ref, amps_ref, own, other, right, total, out_ref, sems,
):
    nq, nv, _ = own.shape
    half, part = nv // 2, nq // 2
    slots = other.shape[1]
    aux, core, x0, y0 = (place_ref[i] for i in range(4))

    fetch = pltpu.make_async_copy(got_hbm, got_ref, sems.at[nq])
    fetch.start()
    own_copies = [pltpu.make_async_copy(own_hbm.at[q], own.at[q], sems.at[q]) for q in range(nq)]
    for copy in own_copies:
        copy.start()
    for h in range(2):
        for owner, src in ((core, near_hbm), (1 - core, far_hbm)):
            for outer in range(SIDE):
                for inner in range(SIDE):
                    dx = inner + owner * (outer - inner)
                    dy = outer + owner * (inner - outer)
                    x, y = lax.rem(x0 + SIDE - dx, SIDE), lax.rem(y0 + SIDE - dy, SIDE)
                    pltpu.make_async_copy(
                        src.at[outer, inner, pl.ds(h * part, part)],
                        other.at[pl.ds(h * part, part), (owner * SIDE + x) * SIDE + y],
                        sems.at[nq + 1 + h],
                    ).start()
    fetch.wait()

    couples, _, both, _ = got_ref.shape
    chunk = couples // 8
    for i in range(8):
        tiles = [got_ref[pl.ds(i * chunk, chunk), side, :, :nv].astype(jnp.float32) for side in range(2)]
        for p, tile in enumerate(split_pairs(*tiles)):
            rows = chunk * both
            amps_ref[p * nv + i * rows : p * nv + (i + 1) * rows] = tile.reshape(rows, nv).astype(jnp.bfloat16)

    def ready(q):
        if q < nq:
            own_copies[q].wait()
        elif (q - nq) % part == 0:
            block = other.at[pl.ds(q - nq, part)]
            pltpu.make_async_copy(block, block, sems.at[nq + 1 + (q - nq) // part]).wait()

    def columns(q):
        if q < nq:
            return own[q, pl.ds(pl.multiple_of(aux * half, half), half), :]
        return other[q - nq, pl.ds(aux * (slots // 2), slots // 2)].reshape(half, nv)

    def vector(q):
        return own[q] if q < nq else other[q - nq].reshape(nv, nv)

    ready(0)
    right[0] = turned(amps_ref, columns(0))
    for q in range(2 * nq):
        if q + 1 < 2 * nq:
            ready(q + 1)
            right[(q + 1) % 2] = turned(amps_ref, columns(q + 1))
        product = jnp.dot(vector(q), right[q % 2], preferred_element_type=jnp.float32)
        total[...] = total[...] + product if q else product

    level = rows_ref[...] + cols_ref[...]
    tiles = [got_ref[:, side, :, nv:].astype(jnp.float32) for side in range(2)]
    stores = []
    for p, hole in enumerate(split_pairs(*tiles)):
        value = hole.reshape(nv, half) + total[:, p * half : (p + 1) * half]
        out_ref[p] = value / (level - occ_ref[p])
        stores.append(pltpu.make_async_copy(out_ref.at[p], out_hbm.at[p], sems.at[p]))
        stores[p].start()
    for store in stores:
        store.wait()


def particle(place, occ_sum, got, own, near, far, rows, cols):
    nq, nv, _ = own.shape
    slots = nv // near.shape[3]
    vmem = pl.BlockSpec(memory_space=pltpu.VMEM)
    smem = pl.BlockSpec(memory_space=pltpu.SMEM)
    anywhere = pl.BlockSpec(memory_space=pl.ANY)
    return pl.pallas_call(
        particle_kernel,
        in_specs=[smem, smem, anywhere, anywhere, anywhere, anywhere, vmem, vmem],
        out_specs=anywhere,
        out_shape=jax.ShapeDtypeStruct((2, nv, nv // 2), jnp.float32),
        scratch_shapes=[
            pltpu.VMEM(got.shape, jnp.bfloat16),
            pltpu.VMEM((2 * nv, nv), jnp.bfloat16),
            pltpu.VMEM((nq, nv, nv), jnp.bfloat16),
            pltpu.VMEM((nq, slots, nv // slots, nv), jnp.bfloat16),
            pltpu.VMEM((2, nv, nv), jnp.bfloat16),
            pltpu.VMEM((nv, nv), jnp.float32),
            pltpu.VMEM((2, nv, nv // 2), jnp.float32),
            pltpu.SemaphoreType.DMA((nq + 3,)),
        ],
        compiler_params=pltpu.CompilerParams(vmem_limit_bytes=VMEM_LIMIT),
        cost_estimate=pl.CostEstimate(
            flops=8 * nq * nv**3, bytes_accessed=4 * nq * nv * nv, transcendentals=0
        ),
        name="particle",
    )(place, occ_sum, got, own, near, far, rows, cols)


def plane_shift(block, shift, first_core_axis):
    pairs = []
    for x in range(SIDE):
        for y in range(SIDE):
            for core in range(2):
                if core == first_core_axis:
                    to = x * SIDE + (y + shift) % SIDE
                else:
                    to = (x + shift) % SIDE * SIDE + y
                pairs.append(((x * SIDE + y) * 2 + core, to * 2 + core))
    return lax.ppermute(block, ("x", "y", "core"), pairs)


def gather_plane(block):
    for stage in range(2):
        block = jnp.stack([block] + [plane_shift(block, d, 1 - stage) for d in (1, 2, 3)])
    return block


def shards(amplitudes, ladder, cholesky, pair_ids, occ_energy, vir_energy):
    n_pair, rows, n_virt = amplitudes.shape
    half_width = n_virt // lax.axis_size("aux")
    aux, core = lax.axis_index("aux"), lax.axis_index("core")
    x, y = lax.axis_index("x"), lax.axis_index("y")
    strip = half_width // (SIDE * SIDE)

    slot = (core * SIDE + x) * SIDE + y
    piece = lax.dynamic_slice_in_dim(cholesky, slot * strip, strip, 1)
    piece = lax.ppermute(piece, "aux", [(0, 1), (1, 0)])

    mine = lax.dynamic_slice_in_dim(amplitudes, aux * half_width, half_width, 2)
    hole = jnp.dot(
        ladder, mine.reshape(n_pair, -1), preferred_element_type=jnp.float32
    ).astype(jnp.bfloat16)
    packed = jnp.concatenate(
        [amplitudes.reshape(-1, 2 * rows, n_virt), hole.reshape(-1, 2 * rows, half_width)], axis=2
    )
    got = lax.all_to_all(packed, PAIR, split_axis=0, concat_axis=0, tiled=True)
    got = got.reshape(-1, 2, *got.shape[1:])
    near = gather_plane(piece)
    far = lax.ppermute(near, "core", [(0, 1), (1, 0)])

    orbitals = jnp.arange(NO, dtype=jnp.int32)
    first_hot = (pair_ids[:, None] // NO == orbitals[None, :]).astype(jnp.float32)
    second_hot = (pair_ids[:, None] % NO == orbitals[None, :]).astype(jnp.float32)
    occ_sum = jnp.sum((first_hot + second_hot) * occ_energy[None, :], axis=1)
    vir_cols = lax.dynamic_slice_in_dim(vir_energy, aux * half_width, half_width, 0)
    place = jnp.stack([aux, core, x, y]).astype(jnp.int32)

    return particle(place, occ_sum, got, cholesky, near, far, vir_energy[:, None], vir_cols[None, :])


def solution(mesh):
    fine = Mesh(mesh.devices.reshape(SIDE, SIDE, SIDE, 2, 2), AXES)
    in_specs = (P(None, PAIR, None), P(), P("aux", None, None), P(PAIR), P(), P())
    out_specs = P(PAIR, None, "aux")
    return jax.shard_map(shards, mesh=fine, in_specs=in_specs, out_specs=out_specs, check_vma=False)
```

```python
import jax
import jax.numpy as jnp
from jax import lax
from jax.experimental import pallas as pl
from jax.experimental.pallas import tpu as pltpu
from jax.sharding import Mesh, PartitionSpec as P

NO = 16
AXES = ("x", "y", "z", "core", "aux")
PAIR = AXES[:4]
SIDE = 4
VMEM_LIMIT = 56 * 1024 * 1024
NT = (((1,), (1,)), ((), ()))


def turned(amps_ref, cols):
    nv = cols.shape[1]
    return jnp.concatenate(
        [
            lax.dot_general(amps_ref[p * nv : (p + 1) * nv], cols, NT, preferred_element_type=jnp.float32).astype(jnp.bfloat16)
            for p in range(2)
        ],
        axis=1,
    )


def split_pairs(first, second):
    rows = first.shape[1] // 2
    low = lax.broadcasted_iota(jnp.int32, first.shape, 1) < rows
    return (
        jnp.where(low, first, pltpu.roll(second, rows, axis=1)),
        jnp.where(low, pltpu.roll(first, rows, axis=1), second),
    )


def particle_kernel(
    place_ref, occ_ref, got_hbm, own_hbm, near_hbm, far_hbm, rows_ref, cols_ref, out_hbm,
    got_ref, amps_ref, own, other, right, total, out_ref, sems,
):
    nq, nv, _ = own.shape
    half, part = nv // 2, nq // 2
    slots = other.shape[1]
    aux, core, x0, y0 = (place_ref[i] for i in range(4))

    fetches = [
        pltpu.make_async_copy(got_hbm.at[:, side], got_ref.at[:, which], sems.at[index])
        for side, which, index in ((0, core, nq), (1, 1 - core, nq + 3))
    ]
    for fetch in fetches:
        fetch.start()
    own_copies = [pltpu.make_async_copy(own_hbm.at[q], own.at[q], sems.at[q]) for q in range(nq)]
    for copy in own_copies:
        copy.start()
    for h in range(2):
        for owner, src in ((core, near_hbm), (1 - core, far_hbm)):
            for outer in range(SIDE):
                for inner in range(SIDE):
                    dx = inner + owner * (outer - inner)
                    dy = outer + owner * (inner - outer)
                    x, y = lax.rem(x0 + SIDE - dx, SIDE), lax.rem(y0 + SIDE - dy, SIDE)
                    pltpu.make_async_copy(
                        src.at[outer, inner, pl.ds(h * part, part)],
                        other.at[pl.ds(h * part, part), (owner * SIDE + x) * SIDE + y],
                        sems.at[nq + 1 + h],
                    ).start()
    for fetch in fetches:
        fetch.wait()

    couples, _, both, _ = got_ref.shape
    chunk = couples // 8
    for i in range(8):
        tiles = [got_ref[pl.ds(i * chunk, chunk), side, :, :nv].astype(jnp.float32) for side in range(2)]
        for p, tile in enumerate(split_pairs(*tiles)):
            rows = chunk * both
            amps_ref[p * nv + i * rows : p * nv + (i + 1) * rows] = tile.reshape(rows, nv).astype(jnp.bfloat16)

    def ready(q):
        if q < nq:
            own_copies[q].wait()
        elif (q - nq) % part == 0:
            block = other.at[pl.ds(q - nq, part)]
            pltpu.make_async_copy(block, block, sems.at[nq + 1 + (q - nq) // part]).wait()

    def columns(q):
        if q < nq:
            return own[q, pl.ds(pl.multiple_of(aux * half, half), half), :]
        return other[q - nq, pl.ds(aux * (slots // 2), slots // 2)].reshape(half, nv)

    def vector(q):
        return own[q] if q < nq else other[q - nq].reshape(nv, nv)

    ready(0)
    right[0] = turned(amps_ref, columns(0))
    for q in range(2 * nq):
        if q + 1 < 2 * nq:
            ready(q + 1)
            right[(q + 1) % 2] = turned(amps_ref, columns(q + 1))
        product = jnp.dot(vector(q), right[q % 2], preferred_element_type=jnp.float32)
        total[...] = total[...] + product if q else product

    level = rows_ref[...] + cols_ref[...]
    tiles = [got_ref[:, side, :, nv:].astype(jnp.float32) for side in range(2)]
    stores = []
    for p, hole in enumerate(split_pairs(*tiles)):
        value = hole.reshape(nv, half) + total[:, p * half : (p + 1) * half]
        out_ref[p] = value / (level - occ_ref[p])
        stores.append(pltpu.make_async_copy(out_ref.at[p], out_hbm.at[p], sems.at[p]))
        stores[p].start()
    for store in stores:
        store.wait()


def particle(place, occ_sum, got, own, near, far, rows, cols):
    nq, nv, _ = own.shape
    slots = nv // near.shape[3]
    vmem = pl.BlockSpec(memory_space=pltpu.VMEM)
    smem = pl.BlockSpec(memory_space=pltpu.SMEM)
    anywhere = pl.BlockSpec(memory_space=pl.ANY)
    return pl.pallas_call(
        particle_kernel,
        in_specs=[smem, smem, anywhere, anywhere, anywhere, anywhere, vmem, vmem],
        out_specs=anywhere,
        out_shape=jax.ShapeDtypeStruct((2, nv, nv // 2), jnp.float32),
        scratch_shapes=[
            pltpu.VMEM(got.shape, jnp.bfloat16),
            pltpu.VMEM((2 * nv, nv), jnp.bfloat16),
            pltpu.VMEM((nq, nv, nv), jnp.bfloat16),
            pltpu.VMEM((nq, slots, nv // slots, nv), jnp.bfloat16),
            pltpu.VMEM((2, nv, nv), jnp.bfloat16),
            pltpu.VMEM((nv, nv), jnp.float32),
            pltpu.VMEM((2, nv, nv // 2), jnp.float32),
            pltpu.SemaphoreType.DMA((nq + 4,)),
        ],
        compiler_params=pltpu.CompilerParams(vmem_limit_bytes=VMEM_LIMIT),
        cost_estimate=pl.CostEstimate(
            flops=8 * nq * nv**3, bytes_accessed=4 * nq * nv * nv, transcendentals=0
        ),
        name="particle",
    )(place, occ_sum, got, own, near, far, rows, cols)


def plane_shift(block, shift, first_core_axis):
    pairs = []
    for x in range(SIDE):
        for y in range(SIDE):
            for core in range(2):
                if core == first_core_axis:
                    to = x * SIDE + (y + shift) % SIDE
                else:
                    to = (x + shift) % SIDE * SIDE + y
                pairs.append(((x * SIDE + y) * 2 + core, to * 2 + core))
    return lax.ppermute(block, ("x", "y", "core"), pairs)


def gather_plane(block):
    for stage in range(2):
        block = jnp.stack([block] + [plane_shift(block, d, 1 - stage) for d in (1, 2, 3)])
    return block


def windows():
    groups = []
    for core in range(2):
        for first in (2 * core, 2 * core + SIDE):
            run = sorted(((first + i) % (2 * SIDE) for i in range(SIDE)), key=lambda z8: z8 % SIDE)
            groups.append([
                ((cell * SIDE + z8 % SIDE) * 2 + core) * 2 + z8 // SIDE for cell in range(SIDE * SIDE) for z8 in run
            ])
    return groups


def shards(amplitudes, ladder, cholesky, pair_ids, occ_energy, vir_energy):
    n_pair, rows, n_virt = amplitudes.shape
    half_width = n_virt // lax.axis_size("aux")
    aux, core = lax.axis_index("aux"), lax.axis_index("core")
    x, y, z = lax.axis_index("x"), lax.axis_index("y"), lax.axis_index("z")
    strip = half_width // (SIDE * SIDE)

    slot = (core * SIDE + x) * SIDE + y
    piece = lax.dynamic_slice_in_dim(cholesky, slot * strip, strip, 1)
    piece = lax.ppermute(piece, "aux", [(0, 1), (1, 0)])

    hole = jnp.dot(
        ladder, amplitudes.reshape(n_pair, -1), preferred_element_type=jnp.float32
    ).astype(jnp.bfloat16)
    blocks = (SIDE**3, 2, 2 * rows)
    hole = hole.reshape(SIDE * SIDE, SIDE, *blocks[1:], n_virt)
    ring = aux * SIDE + z
    shifted = jnp.logical_and(ring >= 2, ring < 6) == (jnp.arange(SIDE) < 2)
    upper = jnp.stack([jnp.broadcast_to(aux == 1, (SIDE,)), shifted], axis=1)
    hole = jnp.where(upper[None, :, :, None, None], hole[..., half_width:], hole[..., :half_width])
    packed = jnp.concatenate([amplitudes.reshape(*blocks, n_virt), hole.reshape(*blocks, half_width)], axis=3)
    kept = lax.dynamic_slice_in_dim(packed, core, 1, 1)
    passed = lax.ppermute(lax.dynamic_slice_in_dim(packed, 1 - core, 1, 1), "core", [(0, 1), (1, 0)])
    packed = jnp.concatenate([kept, passed], axis=1)
    got = lax.all_to_all(
        packed, AXES, split_axis=0, concat_axis=0, tiled=True, axis_index_groups=windows()
    )
    near = gather_plane(piece)
    far = lax.ppermute(near, "core", [(0, 1), (1, 0)])

    orbitals = jnp.arange(NO, dtype=jnp.int32)
    first_hot = (pair_ids[:, None] // NO == orbitals[None, :]).astype(jnp.float32)
    second_hot = (pair_ids[:, None] % NO == orbitals[None, :]).astype(jnp.float32)
    occ_sum = jnp.sum((first_hot + second_hot) * occ_energy[None, :], axis=1)
    vir_cols = lax.dynamic_slice_in_dim(vir_energy, aux * half_width, half_width, 0)
    place = jnp.stack([aux, core, x, y]).astype(jnp.int32)

    return particle(place, occ_sum, got, cholesky, near, far, vir_energy[:, None], vir_cols[None, :])


def solution(mesh):
    fine = Mesh(mesh.devices.reshape(SIDE, SIDE, SIDE, 2, 2), AXES)
    in_specs = (P(None, PAIR, None), P(), P("aux", None, None), P(PAIR), P(), P())
    out_specs = P(PAIR, None, "aux")
    return jax.shard_map(shards, mesh=fine, in_specs=in_specs, out_specs=out_specs, check_vma=False)
```

```python
import jax
import jax.numpy as jnp
from jax import lax
from jax.experimental import pallas as pl
from jax.experimental.pallas import tpu as pltpu
from jax.sharding import Mesh, PartitionSpec as P

NO = 16
AXES = ("x", "y", "z", "core", "aux")
PAIR = AXES[:4]
SIDE = 4
VMEM_LIMIT = 56 * 1024 * 1024
NT = (((1,), (1,)), ((), ()))


def turned(amps_ref, cols):
    nv = cols.shape[1]
    return jnp.concatenate(
        [
            lax.dot_general(amps_ref[p * nv : (p + 1) * nv], cols, NT, preferred_element_type=jnp.float32).astype(jnp.bfloat16)
            for p in range(2)
        ],
        axis=1,
    )


def split_pairs(first, second):
    rows = first.shape[1] // 2
    low = lax.broadcasted_iota(jnp.int32, first.shape, 1) < rows
    return (
        jnp.where(low, first, pltpu.roll(second, rows, axis=1)),
        jnp.where(low, pltpu.roll(first, rows, axis=1), second),
    )


def particle_kernel(
    place_ref, occ_ref, got_hbm, own_hbm, near_hbm, far_hbm, rows_ref, cols_ref, out_hbm,
    got_ref, amps_ref, own, other, right, total, out_ref, sems,
):
    nq, nv, _ = own.shape
    half, part = nv // 2, nq // 2
    slots = other.shape[1]
    aux, core, x0, y0 = (place_ref[i] for i in range(4))

    fetches = [
        pltpu.make_async_copy(got_hbm.at[:, side], got_ref.at[:, which], sems.at[index])
        for side, which, index in ((0, core, nq), (1, 1 - core, nq + 3))
    ]
    for fetch in fetches:
        fetch.start()
    own_copies = [pltpu.make_async_copy(own_hbm.at[q], own.at[q], sems.at[q]) for q in range(nq)]
    for copy in own_copies:
        copy.start()
    for h in range(2):
        for owner, src in ((core, near_hbm), (1 - core, far_hbm)):
            for outer in range(SIDE):
                for inner in range(SIDE):
                    dx = inner + owner * (outer - inner)
                    dy = outer + owner * (inner - outer)
                    x, y = lax.rem(x0 + SIDE - dx, SIDE), lax.rem(y0 + SIDE - dy, SIDE)
                    pltpu.make_async_copy(
                        src.at[outer, inner, pl.ds(h * part, part)],
                        other.at[pl.ds(h * part, part), (owner * SIDE + x) * SIDE + y],
                        sems.at[nq + 1 + h],
                    ).start()
    for fetch in fetches:
        fetch.wait()

    couples, _, both, _ = got_ref.shape
    chunk = couples // 8
    for i in range(8):
        tiles = [got_ref[pl.ds(i * chunk, chunk), side, :, :nv].astype(jnp.float32) for side in range(2)]
        for p, tile in enumerate(split_pairs(*tiles)):
            rows = chunk * both
            amps_ref[p * nv + i * rows : p * nv + (i + 1) * rows] = tile.reshape(rows, nv).astype(jnp.bfloat16)

    def ready(q):
        if q < nq:
            own_copies[q].wait()
        elif (q - nq) % part == 0:
            block = other.at[pl.ds(q - nq, part)]
            pltpu.make_async_copy(block, block, sems.at[nq + 1 + (q - nq) // part]).wait()

    def columns(q):
        if q < nq:
            return own[q, pl.ds(pl.multiple_of(aux * half, half), half), :]
        return other[q - nq, pl.ds(aux * (slots // 2), slots // 2)].reshape(half, nv)

    def vector(q):
        return own[q] if q < nq else other[q - nq].reshape(nv, nv)

    ready(0)
    right[0] = turned(amps_ref, columns(0))
    for q in range(2 * nq):
        if q + 1 < 2 * nq:
            ready(q + 1)
            right[(q + 1) % 2] = turned(amps_ref, columns(q + 1))
        product = jnp.dot(vector(q), right[q % 2], preferred_element_type=jnp.float32)
        total[...] = total[...] + product if q else product

    level = rows_ref[...] + cols_ref[...]
    tiles = [got_ref[:, side, :, nv:].astype(jnp.float32) for side in range(2)]
    stores = []
    for p, hole in enumerate(split_pairs(*tiles)):
        value = hole.reshape(nv, half) + total[:, p * half : (p + 1) * half]
        out_ref[p] = value / (level - occ_ref[p])
        stores.append(pltpu.make_async_copy(out_ref.at[p], out_hbm.at[p], sems.at[p]))
        stores[p].start()
    for store in stores:
        store.wait()


def particle(place, occ_sum, got, own, near, far, rows, cols):
    nq, nv, _ = own.shape
    slots = nv // near.shape[3]
    vmem = pl.BlockSpec(memory_space=pltpu.VMEM)
    smem = pl.BlockSpec(memory_space=pltpu.SMEM)
    anywhere = pl.BlockSpec(memory_space=pl.ANY)
    return pl.pallas_call(
        particle_kernel,
        in_specs=[smem, smem, anywhere, anywhere, anywhere, anywhere, vmem, vmem],
        out_specs=anywhere,
        out_shape=jax.ShapeDtypeStruct((2, nv, nv // 2), jnp.float32),
        scratch_shapes=[
            pltpu.VMEM(got.shape, jnp.bfloat16),
            pltpu.VMEM((2 * nv, nv), jnp.bfloat16),
            pltpu.VMEM((nq, nv, nv), jnp.bfloat16),
            pltpu.VMEM((nq, slots, nv // slots, nv), jnp.bfloat16),
            pltpu.VMEM((2, nv, nv), jnp.bfloat16),
            pltpu.VMEM((nv, nv), jnp.float32),
            pltpu.VMEM((2, nv, nv // 2), jnp.float32),
            pltpu.SemaphoreType.DMA((nq + 4,)),
        ],
        compiler_params=pltpu.CompilerParams(vmem_limit_bytes=VMEM_LIMIT),
        cost_estimate=pl.CostEstimate(
            flops=8 * nq * nv**3, bytes_accessed=4 * nq * nv * nv, transcendentals=0
        ),
        name="particle",
    )(place, occ_sum, got, own, near, far, rows, cols)


def plane_shift(block, shift, first_core_axis):
    pairs = []
    for x in range(SIDE):
        for y in range(SIDE):
            for core in range(2):
                if core == first_core_axis:
                    to = x * SIDE + (y + shift) % SIDE
                else:
                    to = (x + shift) % SIDE * SIDE + y
                pairs.append(((x * SIDE + y) * 2 + core, to * 2 + core))
    return lax.ppermute(block, ("x", "y", "core"), pairs)


def gather_stage(block, stage):
    return jnp.stack([block] + [plane_shift(block, d, 1 - stage) for d in range(1, SIDE)])


def windows():
    groups = []
    for core in range(2):
        for first in (2 * core, 2 * core + SIDE):
            run = sorted(((first + i) % (2 * SIDE) for i in range(SIDE)), key=lambda z8: z8 % SIDE)
            groups.append([
                ((cell * SIDE + z8 % SIDE) * 2 + core) * 2 + z8 // SIDE for cell in range(SIDE * SIDE) for z8 in run
            ])
    return groups


def shards(amplitudes, ladder, cholesky, pair_ids, occ_energy, vir_energy):
    n_pair, rows, n_virt = amplitudes.shape
    half_width = n_virt // lax.axis_size("aux")
    aux, core = lax.axis_index("aux"), lax.axis_index("core")
    x, y, z = lax.axis_index("x"), lax.axis_index("y"), lax.axis_index("z")
    strip = half_width // (SIDE * SIDE)

    slot = (core * SIDE + x) * SIDE + y
    piece = lax.dynamic_slice_in_dim(cholesky, slot * strip, strip, 1)
    piece = lax.ppermute(piece, "aux", [(0, 1), (1, 0)])

    hole = jnp.dot(
        ladder, amplitudes.reshape(n_pair, -1), preferred_element_type=jnp.float32
    ).astype(jnp.bfloat16)
    blocks = (SIDE**3, 2, 2 * rows)
    hole = hole.reshape(SIDE * SIDE, SIDE, *blocks[1:], n_virt)
    ring = aux * SIDE + z
    shifted = jnp.logical_and(ring >= 2, ring < 6) == (jnp.arange(SIDE) < 2)
    upper = jnp.stack([jnp.broadcast_to(aux == 1, (SIDE,)), shifted], axis=1)
    hole = jnp.where(upper[None, :, :, None, None], hole[..., half_width:], hole[..., :half_width])
    packed = jnp.concatenate([amplitudes.reshape(*blocks, n_virt), hole.reshape(*blocks, half_width)], axis=3)
    kept = lax.dynamic_slice_in_dim(packed, core, 1, 1)
    passed, piece = lax.optimization_barrier((lax.dynamic_slice_in_dim(packed, 1 - core, 1, 1), piece))
    passed = lax.ppermute(passed, "core", [(0, 1), (1, 0)])
    packed = jnp.concatenate([kept, passed], axis=1)
    packed, first = lax.optimization_barrier((packed, gather_stage(piece, 0)))
    got = lax.all_to_all(
        packed, AXES, split_axis=0, concat_axis=0, tiled=True, axis_index_groups=windows()
    )
    near = gather_stage(first, 1)
    far = lax.ppermute(near, "core", [(0, 1), (1, 0)])

    orbitals = jnp.arange(NO, dtype=jnp.int32)
    first_hot = (pair_ids[:, None] // NO == orbitals[None, :]).astype(jnp.float32)
    second_hot = (pair_ids[:, None] % NO == orbitals[None, :]).astype(jnp.float32)
    occ_sum = jnp.sum((first_hot + second_hot) * occ_energy[None, :], axis=1)
    vir_cols = lax.dynamic_slice_in_dim(vir_energy, aux * half_width, half_width, 0)
    place = jnp.stack([aux, core, x, y]).astype(jnp.int32)

    return particle(place, occ_sum, got, cholesky, near, far, vir_energy[:, None], vir_cols[None, :])


def solution(mesh):
    fine = Mesh(mesh.devices.reshape(SIDE, SIDE, SIDE, 2, 2), AXES)
    in_specs = (P(None, PAIR, None), P(), P("aux", None, None), P(PAIR), P(), P())
    out_specs = P(PAIR, None, "aux")
    return jax.shard_map(shards, mesh=fine, in_specs=in_specs, out_specs=out_specs, check_vma=False)
```

```python
import jax
import jax.numpy as jnp
from jax import lax
from jax.experimental import pallas as pl
from jax.experimental.pallas import tpu as pltpu
from jax.sharding import Mesh, PartitionSpec as P

NO = 16
AXES = ("x", "y", "z", "core", "aux")
PAIR = AXES[:4]
SIDE = 4
OWN_LIMIT = 48 * 1024 * 1024
OTHER_LIMIT = 48 * 1024 * 1024
NT = (((1,), (1,)), ((), ()))


def turned(amps_ref, cols):
    nv = cols.shape[1]
    return jnp.concatenate(
        [
            lax.dot_general(amps_ref[p * nv : (p + 1) * nv], cols, NT, preferred_element_type=jnp.float32).astype(jnp.bfloat16)
            for p in range(2)
        ],
        axis=1,
    )


def split_pairs(first, second):
    rows = first.shape[1] // 2
    low = lax.broadcasted_iota(jnp.int32, first.shape, 1) < rows
    return (
        jnp.where(low, first, pltpu.roll(second, rows, axis=1)),
        jnp.where(low, pltpu.roll(first, rows, axis=1), second),
    )


def add_vectors(nq, ready, vector, columns, amps_ref, right, total, started):
    ready(0)
    right[0] = turned(amps_ref, columns(0))
    for q in range(nq):
        if q + 1 < nq:
            ready(q + 1)
            right[(q + 1) % 2] = turned(amps_ref, columns(q + 1))
        product = jnp.dot(vector(q), right[q % 2], preferred_element_type=jnp.float32)
        total[...] = total[...] + product if q or started else product


def own_kernel(place_ref, got_hbm, own_hbm, total, amps_ref, got_ref, own, right, sems):
    nq, nv, _ = own.shape
    half = nv // 2
    fetches = [
        pltpu.make_async_copy(got_hbm.at[:, side, :, pl.ds(0, nv)], got_ref.at[:, which], sems.at[nq + side])
        for side, which in ((0, place_ref[1]), (1, 1 - place_ref[1]))
    ]
    for fetch in fetches:
        fetch.start()
    copies = [pltpu.make_async_copy(own_hbm.at[q], own.at[q], sems.at[q]) for q in range(nq)]
    for copy in copies:
        copy.start()
    for fetch in fetches:
        fetch.wait()
    couples, _, both, _ = got_ref.shape
    chunk = couples // 8
    for i in range(8):
        tiles = [got_ref[pl.ds(i * chunk, chunk), side].astype(jnp.float32) for side in range(2)]
        for p, tile in enumerate(split_pairs(*tiles)):
            rows = chunk * both
            amps_ref[p * nv + i * rows : p * nv + (i + 1) * rows] = tile.reshape(rows, nv).astype(jnp.bfloat16)
    start = pl.multiple_of(place_ref[0] * half, half)
    add_vectors(
        nq, lambda q: copies[q].wait(), lambda q: own[q], lambda q: own[q, pl.ds(start, half), :],
        amps_ref, right, total, False,
    )


def other_kernel(*refs):
    place_ref, occ_ref, got_hbm, base_hbm, amps_hbm = refs[:5]
    sources, (rows_ref, cols_ref, out_hbm) = refs[5:7], refs[7:10]
    got_ref, amps_ref, other, right, total, out_ref, sems = refs[10:]
    nq, slots, _, nv = other.shape
    half, part = nv // 2, nq // 2
    aux, core, x0, y0 = (place_ref[i] for i in range(4))
    load = pltpu.make_async_copy(amps_hbm, amps_ref, sems.at[6])
    load.start()
    for h in range(2):
        for owner, src in ((core, sources[0]), (1 - core, sources[1])):
            for outer in range(SIDE):
                for inner in range(SIDE):
                    dx = inner + owner * (outer - inner)
                    dy = outer + owner * (inner - outer)
                    x, y = lax.rem(x0 + SIDE - dx, SIDE), lax.rem(y0 + SIDE - dy, SIDE)
                    pltpu.make_async_copy(
                        src.at[outer, inner, pl.ds(h * part, part)],
                        other.at[pl.ds(h * part, part), (owner * SIDE + x) * SIDE + y],
                        sems.at[h],
                    ).start()
    fill = pltpu.make_async_copy(base_hbm, total, sems.at[2])
    fill.start()
    fetches = [
        pltpu.make_async_copy(got_hbm.at[:, side, :, pl.ds(nv, half)], got_ref.at[:, which], sems.at[index])
        for side, which, index in ((0, core, 3), (1, 1 - core, 7))
    ]
    for fetch in fetches:
        fetch.start()

    def ready(q):
        if q % part == 0:
            block = other.at[pl.ds(q, part)]
            pltpu.make_async_copy(block, block, sems.at[q // part]).wait()

    fill.wait()
    load.wait()
    add_vectors(
        nq, ready, lambda q: other[q].reshape(nv, nv),
        lambda q: other[q, pl.ds(aux * (slots // 2), slots // 2)].reshape(half, nv),
        amps_ref, right, total, True,
    )
    for fetch in fetches:
        fetch.wait()
    level = rows_ref[...] + cols_ref[...]
    tiles = [got_ref[:, side].astype(jnp.float32) for side in range(2)]
    stores = []
    for p, hole in enumerate(split_pairs(*tiles)):
        value = hole.reshape(nv, half) + total[:, p * half : (p + 1) * half]
        out_ref[p] = value / (level - occ_ref[p])
        stores.append(pltpu.make_async_copy(out_ref.at[p], out_hbm.at[p], sems.at[4 + p]))
        stores[p].start()
    for store in stores:
        store.wait()


def estimate(nq, nv):
    return pl.CostEstimate(flops=4 * nq * nv**3, bytes_accessed=2 * nq * nv * nv, transcendentals=0)


VMEM = pl.BlockSpec(memory_space=pltpu.VMEM)
SMEM = pl.BlockSpec(memory_space=pltpu.SMEM)
ANYWHERE = pl.BlockSpec(memory_space=pl.ANY)


def own_vectors(place, got, own):
    nq, nv, _ = own.shape
    return pl.pallas_call(
        own_kernel,
        in_specs=[SMEM, ANYWHERE, ANYWHERE],
        out_specs=[VMEM, VMEM],
        out_shape=[
            jax.ShapeDtypeStruct((nv, nv), jnp.float32),
            jax.ShapeDtypeStruct((2 * nv, nv), jnp.bfloat16),
        ],
        scratch_shapes=[
            pltpu.VMEM((*got.shape[:3], nv), jnp.bfloat16),
            pltpu.VMEM((nq, nv, nv), jnp.bfloat16),
            pltpu.VMEM((2, nv, nv), jnp.bfloat16),
            pltpu.SemaphoreType.DMA((nq + 2,)),
        ],
        compiler_params=pltpu.CompilerParams(vmem_limit_bytes=OWN_LIMIT),
        cost_estimate=pl.CostEstimate(flops=4 * nq * nv**3 // 16, bytes_accessed=2 * nq * nv * nv // 16, transcendentals=0),
        name="own_vectors",
    )(place, got, own)


def other_vectors(place, occ_sum, got, base, amps, near, far, rows, cols):
    nq, strip, nv = near.shape[2:]
    return pl.pallas_call(
        other_kernel,
        in_specs=[SMEM, SMEM, *[ANYWHERE] * 5, VMEM, VMEM],
        out_specs=ANYWHERE,
        out_shape=jax.ShapeDtypeStruct((2, nv, nv // 2), jnp.float32),
        scratch_shapes=[
            pltpu.VMEM((*got.shape[:3], nv // 2), jnp.bfloat16),
            pltpu.VMEM(amps.shape, jnp.bfloat16),
            pltpu.VMEM((nq, nv // strip, strip, nv), jnp.bfloat16),
            pltpu.VMEM((2, nv, nv), jnp.bfloat16),
            pltpu.VMEM((nv, nv), jnp.float32),
            pltpu.VMEM((2, nv, nv // 2), jnp.float32),
            pltpu.SemaphoreType.DMA((8,)),
        ],
        compiler_params=pltpu.CompilerParams(vmem_limit_bytes=OTHER_LIMIT),
        cost_estimate=estimate(nq, nv),
        name="other_vectors",
    )(place, occ_sum, got, base, amps, near, far, rows, cols)


def plane_shift(block, shift, first_core_axis):
    pairs = []
    for x in range(SIDE):
        for y in range(SIDE):
            for core in range(2):
                if core == first_core_axis:
                    to = x * SIDE + (y + shift) % SIDE
                else:
                    to = (x + shift) % SIDE * SIDE + y
                pairs.append(((x * SIDE + y) * 2 + core, to * 2 + core))
    return lax.ppermute(block, ("x", "y", "core"), pairs)


def gather_stage(block, stage):
    return jnp.stack([block] + [plane_shift(block, d, 1 - stage) for d in range(1, SIDE)])


def windows():
    groups = []
    for core in range(2):
        for first in (2 * core, 2 * core + SIDE):
            run = sorted(((first + i) % (2 * SIDE) for i in range(SIDE)), key=lambda z8: z8 % SIDE)
            groups.append([
                ((cell * SIDE + z8 % SIDE) * 2 + core) * 2 + z8 // SIDE for cell in range(SIDE * SIDE) for z8 in run
            ])
    return groups


def shards(amplitudes, ladder, cholesky, pair_ids, occ_energy, vir_energy):
    n_pair, rows, n_virt = amplitudes.shape
    half_width = n_virt // lax.axis_size("aux")
    aux, core = lax.axis_index("aux"), lax.axis_index("core")
    x, y, z = lax.axis_index("x"), lax.axis_index("y"), lax.axis_index("z")
    strip = half_width // (SIDE * SIDE)

    slot = (core * SIDE + x) * SIDE + y
    piece = lax.dynamic_slice_in_dim(cholesky, slot * strip, strip, 1)
    piece = lax.ppermute(piece, "aux", [(0, 1), (1, 0)])

    hole = jnp.dot(
        ladder, amplitudes.reshape(n_pair, -1), preferred_element_type=jnp.float32
    ).astype(jnp.bfloat16)
    blocks = (SIDE**3, 2, 2 * rows)
    hole = hole.reshape(SIDE * SIDE, SIDE, *blocks[1:], n_virt)
    ring = aux * SIDE + z
    shifted = jnp.logical_and(ring >= 2, ring < 6) == (jnp.arange(SIDE) < 2)
    upper = jnp.stack([jnp.broadcast_to(aux == 1, (SIDE,)), shifted], axis=1)
    hole = jnp.where(upper[None, :, :, None, None], hole[..., half_width:], hole[..., :half_width])
    packed = jnp.concatenate([amplitudes.reshape(*blocks, n_virt), hole.reshape(*blocks, half_width)], axis=3)
    kept = lax.dynamic_slice_in_dim(packed, core, 1, 1)
    passed = lax.ppermute(lax.dynamic_slice_in_dim(packed, 1 - core, 1, 1), "core", [(0, 1), (1, 0)])
    packed = jnp.concatenate([kept, passed], axis=1)
    got = lax.all_to_all(
        packed, AXES, split_axis=0, concat_axis=0, tiled=True, axis_index_groups=windows()
    )
    orbitals = jnp.arange(NO, dtype=jnp.int32)
    first_hot = (pair_ids[:, None] // NO == orbitals[None, :]).astype(jnp.float32)
    second_hot = (pair_ids[:, None] % NO == orbitals[None, :]).astype(jnp.float32)
    occ_sum = jnp.sum((first_hot + second_hot) * occ_energy[None, :], axis=1)
    vir_cols = lax.dynamic_slice_in_dim(vir_energy, aux * half_width, half_width, 0)
    place = jnp.stack([aux, core, x, y]).astype(jnp.int32)

    small = (place, occ_sum, vir_energy[:, None], vir_cols[None, :])
    first, small = lax.optimization_barrier((gather_stage(piece, 0), small))
    near = gather_stage(first, 1)
    far = lax.ppermute(near, "core", [(0, 1), (1, 0)])
    place, occ_sum, rows_energy, cols_energy = small
    base, pair_amps = own_vectors(place, got, cholesky)
    return other_vectors(place, occ_sum, got, base, pair_amps, near, far, rows_energy, cols_energy)


def solution(mesh):
    fine = Mesh(mesh.devices.reshape(SIDE, SIDE, SIDE, 2, 2), AXES)
    in_specs = (P(None, PAIR, None), P(), P("aux", None, None), P(PAIR), P(), P())
    out_specs = P(PAIR, None, "aux")
    return jax.shard_map(shards, mesh=fine, in_specs=in_specs, out_specs=out_specs, check_vma=False)
```

```python
import jax
import jax.numpy as jnp
from jax import lax
from jax.experimental import pallas as pl
from jax.experimental.pallas import tpu as pltpu
from jax.sharding import Mesh, PartitionSpec as P

NO = 16
AXES = ("x", "y", "z", "core", "aux")
PAIR = AXES[:4]
SIDE = 4
VMEM_LIMIT = 48 * 1024 * 1024
NT = (((1,), (1,)), ((), ()))


def turned(amps_ref, cols):
    nv = cols.shape[1]
    return jnp.concatenate(
        [
            lax.dot_general(amps_ref[p * nv : (p + 1) * nv], cols, NT, preferred_element_type=jnp.float32).astype(jnp.bfloat16)
            for p in range(2)
        ],
        axis=1,
    )


def split_pairs(first, second):
    rows = first.shape[1] // 2
    low = lax.broadcasted_iota(jnp.int32, first.shape, 1) < rows
    return (
        jnp.where(low, first, pltpu.roll(second, rows, axis=1)),
        jnp.where(low, pltpu.roll(first, rows, axis=1), second),
    )


def particle_kernel(
    place_ref, occ_ref, got_hbm, own_hbm, near_hbm, far_hbm, rows_ref, cols_ref, out_hbm,
    got_ref, amps_ref, own, other, right, total, out_ref, sems,
):
    nq, nv, _ = own.shape
    half, part = nv // 2, nq // 2
    slots = other.shape[1]
    aux, core, x0, y0 = (place_ref[i] for i in range(4))

    fetch = pltpu.make_async_copy(got_hbm, got_ref, sems.at[nq])
    fetch.start()
    own_copies = [pltpu.make_async_copy(own_hbm.at[q], own.at[q], sems.at[q]) for q in range(nq)]
    for copy in own_copies:
        copy.start()
    for h in range(2):
        for owner, src in ((core, near_hbm), (1 - core, far_hbm)):
            for outer in range(SIDE):
                for inner in range(SIDE):
                    dx = inner + owner * (outer - inner)
                    dy = outer + owner * (inner - outer)
                    x, y = lax.rem(x0 + SIDE - dx, SIDE), lax.rem(y0 + SIDE - dy, SIDE)
                    pltpu.make_async_copy(
                        src.at[outer, inner, pl.ds(h * part, part)],
                        other.at[pl.ds(h * part, part), (owner * SIDE + x) * SIDE + y],
                        sems.at[nq + 1 + h],
                    ).start()
    fetch.wait()

    couples, _, both, _ = got_ref.shape
    chunk = couples // 8
    for i in range(8):
        tiles = [got_ref[pl.ds(i * chunk, chunk), side, :, :nv].astype(jnp.float32) for side in range(2)]
        for p, tile in enumerate(split_pairs(*tiles)):
            rows = chunk * both
            amps_ref[p * nv + i * rows : p * nv + (i + 1) * rows] = tile.reshape(rows, nv).astype(jnp.bfloat16)

    def ready(q):
        if q < nq:
            own_copies[q].wait()
        elif (q - nq) % part == 0:
            block = other.at[pl.ds(q - nq, part)]
            pltpu.make_async_copy(block, block, sems.at[nq + 1 + (q - nq) // part]).wait()

    def columns(q):
        if q < nq:
            return own[q, pl.ds(pl.multiple_of(aux * half, half), half), :]
        return other[q - nq, pl.ds(aux * (slots // 2), slots // 2)].reshape(half, nv)

    def vector(q):
        return own[q] if q < nq else other[q - nq].reshape(nv, nv)

    ready(0)
    right[0] = turned(amps_ref, columns(0))
    for q in range(2 * nq):
        if q + 1 < 2 * nq:
            ready(q + 1)
            right[(q + 1) % 2] = turned(amps_ref, columns(q + 1))
        product = jnp.dot(vector(q), right[q % 2], preferred_element_type=jnp.float32)
        total[...] = total[...] + product if q else product

    level = rows_ref[...] + cols_ref[...]
    tiles = [got_ref[:, side, :, nv:].astype(jnp.float32) for side in range(2)]
    stores = []
    for p, hole in enumerate(split_pairs(*tiles)):
        value = hole.reshape(nv, half) + total[:, p * half : (p + 1) * half]
        out_ref[p] = value / (level - occ_ref[p])
        stores.append(pltpu.make_async_copy(out_ref.at[p], out_hbm.at[p], sems.at[p]))
        stores[p].start()
    for store in stores:
        store.wait()


def particle(place, occ_sum, got, own, near, far, rows, cols):
    nq, nv, _ = own.shape
    slots = nv // near.shape[3]
    vmem = pl.BlockSpec(memory_space=pltpu.VMEM)
    smem = pl.BlockSpec(memory_space=pltpu.SMEM)
    anywhere = pl.BlockSpec(memory_space=pl.ANY)
    return pl.pallas_call(
        particle_kernel,
        in_specs=[smem, smem, anywhere, anywhere, anywhere, anywhere, vmem, vmem],
        out_specs=anywhere,
        out_shape=jax.ShapeDtypeStruct((2, nv, nv // 2), jnp.float32),
        scratch_shapes=[
            pltpu.VMEM(got.shape, jnp.bfloat16),
            pltpu.VMEM((2 * nv, nv), jnp.bfloat16),
            pltpu.VMEM((nq, nv, nv), jnp.bfloat16),
            pltpu.VMEM((nq, slots, nv // slots, nv), jnp.bfloat16),
            pltpu.VMEM((2, nv, nv), jnp.bfloat16),
            pltpu.VMEM((nv, nv), jnp.float32),
            pltpu.VMEM((2, nv, nv // 2), jnp.float32),
            pltpu.SemaphoreType.DMA((nq + 3,)),
        ],
        compiler_params=pltpu.CompilerParams(vmem_limit_bytes=VMEM_LIMIT),
        cost_estimate=pl.CostEstimate(
            flops=8 * nq * nv**3, bytes_accessed=4 * nq * nv * nv, transcendentals=0
        ),
        name="particle",
    )(place, occ_sum, got, own, near, far, rows, cols)


def plane_shift(block, shift, first_core_axis):
    pairs = []
    for x in range(SIDE):
        for y in range(SIDE):
            for core in range(2):
                if core == first_core_axis:
                    to = x * SIDE + (y + shift) % SIDE
                else:
                    to = (x + shift) % SIDE * SIDE + y
                pairs.append(((x * SIDE + y) * 2 + core, to * 2 + core))
    return lax.ppermute(block, ("x", "y", "core"), pairs)


def gather_plane(block):
    for stage in range(2):
        block = jnp.stack([block] + [plane_shift(block, d, 1 - stage) for d in (1, 2, 3)])
    return block


def shards(amplitudes, ladder, cholesky, pair_ids, occ_energy, vir_energy):
    n_pair, rows, n_virt = amplitudes.shape
    half_width = n_virt // lax.axis_size("aux")
    aux, core = lax.axis_index("aux"), lax.axis_index("core")
    x, y = lax.axis_index("x"), lax.axis_index("y")
    strip = half_width // (SIDE * SIDE)

    slot = (core * SIDE + x) * SIDE + y
    piece = lax.dynamic_slice_in_dim(cholesky, slot * strip, strip, 1)
    piece = lax.ppermute(piece, "aux", [(0, 1), (1, 0)])

    mine = lax.dynamic_slice_in_dim(amplitudes, aux * half_width, half_width, 2)
    hole = jnp.dot(
        ladder, mine.reshape(n_pair, -1), preferred_element_type=jnp.float32
    ).astype(jnp.bfloat16)
    packed = jnp.concatenate(
        [amplitudes.reshape(-1, 2 * rows, n_virt), hole.reshape(-1, 2 * rows, half_width)], axis=2
    )
    got = lax.all_to_all(packed, PAIR, split_axis=0, concat_axis=0, tiled=True)
    got = got.reshape(-1, 2, *got.shape[1:])
    near = gather_plane(piece)
    far = lax.ppermute(near, "core", [(0, 1), (1, 0)])

    orbitals = jnp.arange(NO, dtype=jnp.int32)
    first_hot = (pair_ids[:, None] // NO == orbitals[None, :]).astype(jnp.float32)
    second_hot = (pair_ids[:, None] % NO == orbitals[None, :]).astype(jnp.float32)
    occ_sum = jnp.sum((first_hot + second_hot) * occ_energy[None, :], axis=1)
    vir_cols = lax.dynamic_slice_in_dim(vir_energy, aux * half_width, half_width, 0)
    place = jnp.stack([aux, core, x, y]).astype(jnp.int32)

    return particle(place, occ_sum, got, cholesky, near, far, vir_energy[:, None], vir_cols[None, :])


def solution(mesh):
    fine = Mesh(mesh.devices.reshape(SIDE, SIDE, SIDE, 2, 2), AXES)
    in_specs = (P(None, PAIR, None), P(), P("aux", None, None), P(PAIR), P(), P())
    out_specs = P(PAIR, None, "aux")
    return jax.shard_map(shards, mesh=fine, in_specs=in_specs, out_specs=out_specs, check_vma=False)
```
